256 devices in a mesh: rep: 16 (over z_hi, y), tp: 4 (over x), cp: 4 (over z_lo, core).
Axes of the slice: x: 4, y: 4, z: 8 (z_hi: 4, z_lo: 2; z = z_hi * 2 + z_lo), core: 2. Of those that a mesh axis runs over, the one named last changes fastest.
Arguments:
- tokens: bfloat16 [16, 3072, 1280], P('rep', 'cp', 'tp'), may hold values from -6 to 6
- qkv_weight: float32 [1280, 3, 1280], P(('rep', 'cp'), None, 'tp'), may hold values from -0.3 to 0.3
- out_weight: float32 [1280, 1280], P('tp', ('rep', 'cp')), may hold values from -0.3 to 0.3
- gate_up_weight: float32 [1280, 2, 5120], P(('rep', 'cp'), None, 'tp'), may hold values from -0.3 to 0.3
- down_weight: float32 [5120, 1280], P('tp', ('rep', 'cp')), may hold values from -0.15 to 0.15
- qk_scale: float32 [1280], P('tp'), may hold values from 0.9 to 6.6, as said below
- attn_rate: float32 [1280], replicated, may hold values from 0.05 to 0.6
- mlp_rate: float32 [1280], replicated, may hold values from 0.05 to 0.6
- up_scale: float32 [5120], P('tp'), may hold values from 0.5 to 2
- gate_scale: float32 [5120], P('tp'), may hold values from 0.5 to 2
- segment_ids: int32 [16, 3072], P('rep'), may hold values from 0 to 23, never falling along the last dimension, each value on 1 to 512 neighbouring positions
Outputs:
- next_state: bfloat16 [16, 3072, 1280], P('rep', 'cp', 'tp')
The draws below stay inside these ranges and needn't reach their ends.
Inputs may be any that keep to these rules, and one draw needn't show every extreme that they name: `segment_ids`: along each replica's row the ids never fall, and each prompt covers 1 to 512 positions; some prompt covers exactly 512. `qk_scale`: positive channel scales.
All inputs are finite; a program needn't handle non-finite values.
Results may differ from the reference program's by a relative error of at most 0.015.
Values may be sent and summed in bfloat16 or wider, within the bound.
No kernel may reach another device: no remote copies, remote signals or barrier semaphores. Data moves between devices by JAX's collectives and lax.ppermute only.
A program may use at most 128 MiB of HBM per device.

```python
import math
import jax
import jax.numpy as jnp
import numpy as np
from jax import lax

D = 1280
H = 20
HD = 64
FF = 5120
MAXLEN = 512
N_REPLICAS = 16
STREAM = 3072
PROMPTS = 24


def level_line(count):
    return jnp.arange(count, dtype=jnp.float32) / max(count - 1, 1)


def drawn_ramp(count):
    return 0.5 + level_line(count)


def draw_qkv_weight(key, part):
    first, second, third = jax.random.split(jax.random.fold_in(key, 11), 3)
    ramp_rows = drawn_ramp(D)[:, None]
    query_part = 0.03 * jax.random.normal(first, (D, D), jnp.float32)
    key_part = 0.03 * jax.random.normal(second, (D, D), jnp.float32)
    value_part = 0.03 * jax.random.normal(third, (D, D), jnp.float32)
    stacked = jnp.stack([query_part * ramp_rows, key_part * ramp_rows, value_part * ramp_rows], axis=1)
    return jnp.clip(stacked, -0.3, 0.3)


def draw_out_weight(key, part):
    noise_key = jax.random.fold_in(key, 31)
    values = jax.random.normal(noise_key, (D, D), jnp.float32)
    ramp_cols = drawn_ramp(D)[None, :]
    return jnp.clip(values * ramp_cols / math.sqrt(D), -0.3, 0.3)


def draw_gate_up_weight(key, part):
    noise_key = jax.random.fold_in(key, 37)
    values = jax.random.normal(noise_key, (D, 2, FF), jnp.float32)
    ramp_rows = drawn_ramp(D)[:, None, None]
    return jnp.clip(values * ramp_rows / math.sqrt(D), -0.3, 0.3)


def draw_down_weight(key, part):
    noise_key = jax.random.fold_in(key, 41)
    values = jax.random.normal(noise_key, (FF, D), jnp.float32)
    ramp_cols = drawn_ramp(D)[None, :]
    return jnp.clip(values * ramp_cols / math.sqrt(FF), -0.15, 0.15)


def draw_qk_scale(key, part):
    first, second = jax.random.split(jax.random.fold_in(key, 23), 2)
    levels = jax.random.uniform(first, (H,), jnp.float32, 0.0, 1.0)
    head_level = jnp.exp(levels * math.log(2.5))
    gains = jax.random.uniform(second, (H, HD), jnp.float32, 0.9, 1.1)
    return (head_level[:, None] * gains).reshape(H * HD)


def block_scale(key, dims, cuts, smallest, largest):
    loudness, own = 1.0, jax.random.fold_in(key, 6)
    for dim, shards_of in cuts:
        steps = jnp.exp(jax.random.uniform(jax.random.fold_in(own, dim), (shards_of,), jnp.float32, smallest / len(cuts), largest / len(cuts)))
        loudness = loudness * jnp.repeat(steps, dims[dim] // shards_of).reshape([-1 if axis == dim else 1 for axis in range(len(dims))])
    return loudness


def length_profile(count, total, most, lean):
    loads = [(1 << 20) // math.isqrt(standing ** lean) + 1 for standing in range(2, count + 1)]
    rest, holding = total - most - (count - 1), [1] * (count - 1)
    while rest > 0:
        free = [i for i in range(count - 1) if holding[i] < most]
        mass, budget = sum([loads[i] for i in free]), rest
        for i in free:
            more = min(most - holding[i], max(1, budget * loads[i] // mass), rest)
            holding[i] = holding[i] + more
            rest = rest - more
    return np.array([most] + holding)


def ragged_sizes(own_key, number_of, total, most, lean):
    if number_of == 2:
        one = jax.random.randint(own_key, (), max(1, total - most), min(most, total - 1) + 1)
        return jnp.stack([one, total - one])
    lengths = jnp.asarray(length_profile(number_of, total, most, lean), jnp.int32)
    couples = (number_of - 1) // 2
    giver, taker = lengths[1:1 + 2 * couples:2], lengths[2:2 + 2 * couples:2]
    room = jnp.minimum(giver - 1, most - taker)
    passed = jax.random.randint(jax.random.fold_in(own_key, 1), (couples,), 0, 1 << 20) % (room + 1)
    lengths = lengths.at[1:1 + 2 * couples:2].set(giver - passed).at[2:2 + 2 * couples:2].set(taker + passed)
    return lengths[jax.random.permutation(jax.random.fold_in(own_key, 2), number_of)]


def scatter_about(own_key, shape, spread, most, cuts=(), held_as=jnp.bfloat16):
    factor_of = block_scale(own_key, shape, cuts, -0.22, 0.18) if cuts else 1.0
    result = jax.random.normal(own_key, shape, jnp.float32) * spread * factor_of
    return jnp.minimum(jnp.maximum(result, -most), most).astype(held_as)


def setup_inputs(seed: int = 0) -> dict:
    arg_keys = jax.random.split(jax.random.key(seed), 12)
    return {
        "tokens": scatter_about(arg_keys[0], (N_REPLICAS, STREAM, D), 1.0, 6.0, ((0, 16), (1, 4), (2, 4))),
        "qkv_weight": draw_qkv_weight(jax.random.fold_in(arg_keys[11], 71), 0),
        "out_weight": draw_out_weight(jax.random.fold_in(arg_keys[11], 71), 0),
        "gate_up_weight": draw_gate_up_weight(jax.random.fold_in(arg_keys[11], 71), 0),
        "down_weight": draw_down_weight(jax.random.fold_in(arg_keys[11], 71), 0),
        "qk_scale": draw_qk_scale(jax.random.fold_in(arg_keys[11], 71), 0),
        "attn_rate": jnp.clip(jnp.exp(jax.random.uniform(arg_keys[6], (D,), jnp.float32, math.log(0.05), math.log(0.6))), 0.05, 0.6),
        "mlp_rate": jnp.clip(jnp.exp(jax.random.uniform(arg_keys[7], (D,), jnp.float32, math.log(0.05), math.log(0.6))), 0.05, 0.6),
        "up_scale": jnp.clip(jnp.exp(math.log(2.0) - 1.3862944 * jax.random.uniform(arg_keys[8], (FF,), jnp.float32) ** block_scale(arg_keys[8], (FF,), ((0, 4),), -0.2, 0.2)), 0.5, 2.0),
        "gate_scale": jnp.clip(jnp.exp(math.log(2.0) - 1.3862944 * jax.random.uniform(arg_keys[9], (FF,), jnp.float32) ** block_scale(arg_keys[9], (FF,), ((0, 4),), -0.2, 0.2)), 0.5, 2.0),
        "segment_ids": jax.vmap(lambda own: jnp.searchsorted(jnp.cumsum(ragged_sizes(own, PROMPTS, STREAM, MAXLEN, 2)), jnp.arange(STREAM), side="right"))(jax.random.split(arg_keys[10], N_REPLICAS)).reshape((N_REPLICAS, STREAM)).astype(jnp.int32),
    }


def unit_rows(array):
    return array * lax.rsqrt(lax.optimization_barrier(jnp.sum(array * array, axis=-1, keepdims=True)) + 1e-06)

def rotate(array, position):
    half_dim = array.shape[-1] // 2
    frequency = jnp.exp(-math.log(10000.0) * jnp.arange(half_dim, dtype=jnp.float32) * 2.0 / array.shape[-1])
    angles = position.astype(jnp.float32)[:, None] * frequency[None, :]
    cosine = jnp.cos(angles)[:, None, :]
    sine_part = jnp.sin(angles)[:, None, :]
    first_half = array[..., :half_dim]
    second_half = array[..., half_dim:]
    return jnp.concatenate([first_half * cosine - second_half * sine_part, first_half * sine_part + second_half * cosine], axis=-1)

def stream_positions(segment):
    order_index = jnp.arange(segment.shape[0], dtype=jnp.int32)
    earlier = jnp.concatenate([segment[:1], segment[:-1]])
    boundary = jnp.where(segment != earlier, order_index, jnp.zeros_like(order_index))
    return order_index - lax.cummax(boundary)

def reference(tokens, qkv_weight, out_weight, gate_up_weight, down_weight, qk_scale, attn_rate, mlp_rate, up_scale, gate_scale, segment_ids):
    qkv_norm = (qkv_weight * lax.rsqrt(lax.optimization_barrier(jnp.sum(qkv_weight * qkv_weight, axis=0, keepdims=True)) + 1e-06)).astype(jnp.bfloat16).reshape(D, 3 * D)
    out_norm = (out_weight * lax.rsqrt(lax.optimization_barrier(jnp.sum(out_weight * out_weight, axis=1, keepdims=True)) + 1e-06)).astype(jnp.bfloat16)
    gate_up_norm = (gate_up_weight * lax.rsqrt(lax.optimization_barrier(jnp.sum(gate_up_weight * gate_up_weight, axis=0, keepdims=True)) + 1e-06)).astype(jnp.bfloat16).reshape(D, 2 * FF)
    down_norm = (down_weight * lax.rsqrt(lax.optimization_barrier(jnp.sum(down_weight * down_weight, axis=1, keepdims=True)) + 1e-06)).astype(jnp.bfloat16)
    scale_table = qk_scale.reshape(H, HD)

    def replica(inputs):
        stream_tokens, segment = inputs
        length = segment.shape[0]
        state = unit_rows(stream_tokens.astype(jnp.float32))
        projected = jnp.dot(state.astype(jnp.bfloat16), qkv_norm, preferred_element_type=jnp.float32).reshape(length, 3, H, HD)
        query = (scale_table * unit_rows(projected[:, 0])).astype(jnp.bfloat16)
        keys = (scale_table * unit_rows(projected[:, 1])).astype(jnp.bfloat16)
        values = projected[:, 2].astype(jnp.bfloat16)
        position = stream_positions(segment)
        query_rot = rotate(query.astype(jnp.float32), position).astype(jnp.bfloat16)
        keys_rot = rotate(keys.astype(jnp.float32), position).astype(jnp.bfloat16)
        order_index = jnp.arange(length, dtype=jnp.int32)
        allowed = (segment[:, None] == segment[None, :]) & (order_index[:, None] >= order_index[None, :])

        def one_head(head_inputs):
            head_query, head_keys, head_values = head_inputs
            scores = jnp.dot(head_query, head_keys.T, preferred_element_type=jnp.float32) * math.sqrt(HD)
            scores = jnp.where(allowed, scores, -1e+30)
            exponent = jnp.exp(scores - lax.optimization_barrier(jnp.max(scores, axis=-1, keepdims=True)))
            probs = (exponent / lax.optimization_barrier(jnp.sum(exponent, axis=-1, keepdims=True))).astype(jnp.bfloat16)
            return jnp.dot(probs, head_values, preferred_element_type=jnp.float32).astype(jnp.bfloat16)
        heads_out = lax.map(one_head, (query_rot.transpose(1, 0, 2), keys_rot.transpose(1, 0, 2), values.transpose(1, 0, 2)))
        attended = heads_out.transpose(1, 0, 2).reshape(length, D)
        attn_part = jnp.dot(attended, out_norm, preferred_element_type=jnp.float32)
        mixed = unit_rows(state + attn_rate * (unit_rows(attn_part) - state))
        gate_up = jnp.dot(mixed.astype(jnp.bfloat16), gate_up_norm, preferred_element_type=jnp.float32)
        up_branch = gate_up[:, :FF] * up_scale
        gate_branch = gate_up[:, FF:] * gate_scale * math.sqrt(D)
        inner = (up_branch * jax.nn.silu(gate_branch)).astype(jnp.bfloat16)
        mlp_part = jnp.dot(inner, down_norm, preferred_element_type=jnp.float32)
        return (math.sqrt(D) * unit_rows(mixed + mlp_rate * (unit_rows(mlp_part) - mixed))).astype(jnp.bfloat16)
    return lax.map(replica, (tokens, segment_ids))
```

```python
import math

import jax
import jax.numpy as jnp
from jax import lax
from jax.experimental import pallas as pl
from jax.experimental.pallas import tpu as pltpu
from jax.sharding import Mesh, PartitionSpec as P

D = 1280
HD = 64
EPS = 1e-06
F32 = jnp.float32
BF16 = jnp.bfloat16
Z = ("zh", "zl")
BLOCK = 256
LOG2E = 1.4426950408889634


def ring(count, step):
    return [(i, (i + step) % count) for i in range(count)]


def shift(block, axis, count, step):
    return lax.ppermute(block, axis, ring(count, step))


def swap_core(block):
    return lax.ppermute(block, "co", [(0, 1), (1, 0)])


def place(pieces, count):
    whole = jnp.zeros((count,) + pieces[0][0].shape, pieces[0][0].dtype)
    for block, index in pieces:
        whole = lax.dynamic_update_index_in_dim(whole, block, index % count, 0)
    return whole


def gather_four(block, axis, me):
    pieces = [(block, me)]
    for step in (2, 1, 3):
        pieces.append((shift(block, axis, 4, step), me + 4 - step))
    return place(pieces, 4)


def gather_ring_z(block, me):
    ahead = behind = block
    pieces = [(block, me)]
    for step in range(1, 5):
        ahead = shift(ahead, Z, 8, 1)
        pieces.append((ahead, me + 8 - step))
        if step < 4:
            behind = shift(behind, Z, 8, -1)
            pieces.append((behind, me + step))
    return place(pieces, 8)


def merge_core(low, high, core):
    first = core == 0
    got = swap_core(jnp.where(first, high, low))
    mine = jnp.where(first, low, high)
    return jnp.concatenate([jnp.where(first, mine, got), jnp.where(first, got, mine)], axis=0)


def squares(array, axis):
    wide = array.astype(F32)
    return jnp.sum(wide * wide, axis=axis)


def attention_kernel(start_ref, q_ref, k_ref, v_ref, o_ref):
    heads = q_ref.shape[0] // HD
    key_row = lax.broadcasted_iota(jnp.int32, (BLOCK, BLOCK), 0)
    query_col = lax.broadcasted_iota(jnp.int32, (BLOCK, BLOCK), 1)
    causal = key_row <= query_col

    def one_head(head, carry):
        rows = pl.ds(pl.multiple_of(head * HD, HD), HD)
        for part in range(q_ref.shape[1] // BLOCK):
            cols = slice(part * BLOCK, (part + 1) * BLOCK)
            query = q_ref[rows, cols]
            start = start_ref[:, cols]
            scores = []
            for step in range(3):
                base = (part + step) * BLOCK
                keys = k_ref[rows, base : base + BLOCK]
                score = lax.dot_general(
                    keys, query, (((0,), (0,)), ((), ())), preferred_element_type=F32
                )
                allowed = key_row >= start - base
                if step == 2:
                    allowed = allowed & causal
                scores.append(jnp.where(allowed, score, -1e30))
            top = jnp.maximum(jnp.maximum(scores[0], scores[1]), scores[2])
            top = jnp.max(top, axis=0, keepdims=True)
            total = jnp.zeros((1, BLOCK), F32)
            mixed = jnp.zeros((HD, BLOCK), F32)
            for step in range(3):
                base = (part + step) * BLOCK
                weight = jnp.exp2((scores[step] - top) * (math.sqrt(HD) * LOG2E))
                total = total + jnp.sum(weight, axis=0, keepdims=True)
                mixed = mixed + jnp.dot(
                    v_ref[rows, base : base + BLOCK],
                    weight.astype(BF16),
                    preferred_element_type=F32,
                )
            o_ref[rows, cols] = (mixed / total).astype(BF16)
        return carry

    lax.fori_loop(0, heads, one_head, 0)


def attention(start, query, keys, values):
    return pl.pallas_call(
        attention_kernel,
        out_shape=jax.ShapeDtypeStruct(query.shape, BF16),
        in_specs=[pl.BlockSpec(memory_space=pltpu.VMEM)] * 4,
        out_specs=pl.BlockSpec(memory_space=pltpu.VMEM),
        cost_estimate=pl.CostEstimate(flops=800_000_000, bytes_accessed=4_000_000, transcendentals=3_000_000),
        name="attention",
    )(start, query, keys, values)


def stream_starts(segment):
    order = jnp.arange(segment.shape[0], dtype=jnp.int32)
    earlier = jnp.concatenate([segment[:1], segment[:-1]])
    return lax.cummax(jnp.where(segment != earlier, order, jnp.zeros_like(order)))


def inner_order(array):
    shape = array.shape
    parts = array.reshape((shape[0] // 320, 4, 2, 40) + shape[1:])
    return jnp.swapaxes(parts, 1, 2).reshape(shape)


def outer_order(array):
    shape = array.shape
    parts = array.reshape((shape[0] // 320, 2, 4, 40) + shape[1:])
    return jnp.swapaxes(parts, 1, 2).reshape(shape)


def body(
    tokens,
    qkv_weight,
    out_weight,
    gate_up_weight,
    down_weight,
    qk_scale,
    attn_rate,
    mlp_rate,
    up_scale,
    gate_scale,
    segment_ids,
):
    rows = tokens.shape[1]
    local = tokens.shape[2]
    heads = local // HD
    hidden = gate_up_weight.shape[2]
    tp = lax.axis_index("tp")
    core = lax.axis_index("co")
    ring_y = lax.axis_index("y")
    ring_z = lax.axis_index("zh") * 2 + lax.axis_index("zl")
    piece = lax.axis_index("zl") * 2 + core

    own_tokens = inner_order(tokens[0].T)
    features = gather_four(own_tokens, "tp", tp).reshape(D, rows)

    qkv_local = qkv_weight.astype(BF16).reshape(20, 3 * local)
    side = 3 * local // 2
    qkv_block = merge_core(qkv_local[:, :side], qkv_local[:, side:], core)
    qkv_y = gather_four(qkv_block, "y", ring_y).reshape(160, side)
    qkv_half = gather_ring_z(qkv_y, ring_z).reshape(D, side)
    qkv_other = swap_core(qkv_half)
    qkv = jnp.concatenate(
        [
            jnp.where(core == 0, qkv_half, qkv_other),
            jnp.where(core == 0, qkv_other, qkv_half),
        ],
        axis=1,
    )

    out_rows = lax.all_gather(out_weight.T.astype(BF16), "tp", axis=1, tiled=True)
    gate_up = gate_up_weight.astype(BF16)
    down_rows = down_weight.T.astype(BF16)
    half = hidden // 2

    def side_of(which):
        cols = slice(which * half, (which + 1) * half)
        return jnp.concatenate(
            [out_rows[:, cols], gate_up[:, 0, cols], gate_up[:, 1, cols], down_rows[:, cols]], axis=1
        )

    rest_block = merge_core(side_of(0), side_of(1), core)
    rest_y = gather_four(rest_block, "y", ring_y).reshape(160, 4 * half)
    rest_half = lax.all_gather(rest_y, Z, axis=0, tiled=True)
    rest_other = swap_core(rest_half)

    row_scale = lax.rsqrt(squares(features, 0) + EPS)
    raw = lax.dot_general(qkv, features, (((0,), (0,)), ((), ())), preferred_element_type=F32)
    projected = raw * lax.rsqrt(squares(qkv, 0) + EPS)[:, None] * row_scale[None]
    projected = projected.reshape(3, heads, HD, rows)
    scale_table = qk_scale.reshape(heads, HD, 1)

    starts = stream_starts(segment_ids[0])
    own_first = piece * rows
    own_start = lax.dynamic_slice_in_dim(starts, own_first, rows)
    position = own_first + jnp.arange(rows, dtype=jnp.int32) - own_start
    frequency = jnp.exp(-math.log(10000.0) * jnp.arange(HD // 2, dtype=F32) * 2.0 / HD)
    angles = frequency[:, None] * position.astype(F32)[None]
    cosine, sine = jnp.cos(angles)[None], jnp.sin(angles)[None]

    def turned(kind):
        part = projected[kind]
        length = lax.rsqrt(jnp.sum(part * part, axis=1, keepdims=True) + EPS)
        part = (scale_table * (part * length)).astype(BF16).astype(F32)
        first, second = part[:, : HD // 2], part[:, HD // 2 :]
        both = jnp.concatenate(
            [first * cosine - second * sine, first * sine + second * cosine], axis=1
        )
        return both.astype(BF16).reshape(local, rows)

    query, keys = turned(0), turned(1)
    values = projected[2].astype(BF16).reshape(local, rows)
    window = 2 * BLOCK
    own = jnp.concatenate([keys, values], axis=0)
    before = lax.ppermute(own[:, rows - window :], ("zl", "co"), [(i, i + 1) for i in range(3)])
    both = jnp.concatenate([before, own], axis=1)
    local_start = (own_start - own_first + window)[None]
    attended = attention(local_start, query, both[:local], both[local:])

    everyone = gather_four(attended, "tp", tp).reshape(2, 2 * local, rows)
    attn_part = jnp.zeros((D, rows), F32)
    for block, which in ((rest_half, core), (rest_other, 1 - core)):
        weight = block[:, :half]
        weight = (weight * lax.rsqrt(squares(weight, 0) + EPS)[None]).astype(BF16)
        channels = lax.dynamic_index_in_dim(everyone, which, 0, keepdims=False)
        attn_part = attn_part + jnp.dot(weight, channels, preferred_element_type=F32)

    state = features.astype(F32) * row_scale[None]
    attn_step = inner_order(attn_rate)[:, None]
    mlp_step = inner_order(mlp_rate)[:, None]
    attn_unit = attn_part * lax.rsqrt(squares(attn_part, 0) + EPS)[None]
    mixed = state + attn_step * (attn_unit - state)
    mixed = mixed * lax.rsqrt(squares(mixed, 0) + EPS)[None]
    mixed_in = mixed.astype(BF16)

    mlp_part = jnp.zeros((D, rows), F32)
    for block, which in ((rest_half, core), (rest_other, 1 - core)):
        weight = block[:, half : 3 * half]
        size = lax.rsqrt(squares(weight, 0) + EPS)
        both_kinds = lax.dot_general(
            weight, mixed_in, (((0,), (0,)), ((), ())), preferred_element_type=F32
        )
        up_size = size[:half] * lax.dynamic_slice_in_dim(up_scale, which * half, half)
        gate_size = size[half:] * lax.dynamic_slice_in_dim(gate_scale, which * half, half)
        down = block[:, 3 * half :]
        up_size = up_size * lax.rsqrt(squares(down, 0) + EPS)
        gate = both_kinds[half:] * (gate_size * math.sqrt(D))[:, None]
        inner = (both_kinds[:half] * up_size[:, None] * jax.nn.silu(gate)).astype(BF16)
        mlp_part = mlp_part + jnp.dot(down, inner, preferred_element_type=F32)

    blocks = mlp_part.reshape(4, local, rows)
    small = blocks.astype(BF16)
    mlp_block = lax.dynamic_index_in_dim(blocks, tp, 0, keepdims=False)
    for step in (2, 1, 3):
        sent = lax.dynamic_index_in_dim(small, (tp + step) % 4, 0, keepdims=False)
        mlp_block = mlp_block + shift(sent, "tp", 4, step).astype(F32)

    mixed_block = lax.dynamic_slice_in_dim(mixed, tp * local, local, 0)
    step_block = lax.dynamic_slice_in_dim(mlp_step, tp * local, local, 0)
    kept = mixed_block - step_block * mixed_block
    moved = step_block * mlp_block
    sums = jnp.stack(
        [
            squares(mlp_block, 0),
            squares(kept, 0),
            jnp.sum(kept * moved, axis=0),
            squares(moved, 0),
        ]
    )
    sums = sums + shift(sums, "tp", 4, 2)
    sums = sums + shift(sums, "tp", 4, 1)
    pull = lax.rsqrt(sums[0] + EPS)
    length = jnp.maximum(sums[1] + 2.0 * pull * sums[2] + pull * pull * sums[3], 0.0)
    final = math.sqrt(D) * lax.rsqrt(length + EPS)
    result = (kept + pull[None] * moved) * final[None]
    return outer_order(result).astype(BF16).T[None]


def solution(mesh):
    fine = Mesh(mesh.devices.reshape(4, 4, 4, 2, 2), ("zh", "y", "tp", "zl", "co"))
    rep, cp = ("zh", "y"), ("zl", "co")
    in_specs = (
        P(rep, cp, "tp"),
        P(rep + cp, None, "tp"),
        P("tp", rep + cp),
        P(rep + cp, None, "tp"),
        P("tp", rep + cp),
        P("tp"),
        P(),
        P(),
        P("tp"),
        P("tp"),
        P(rep, None),
    )
    return jax.shard_map(
        body, mesh=fine, in_specs=in_specs, out_specs=P(rep, cp, "tp"), check_vma=False
    )
```

```python
import math

import jax
import jax.numpy as jnp
from jax import lax
from jax.experimental import pallas as pl
from jax.experimental.pallas import tpu as pltpu
from jax.sharding import Mesh, PartitionSpec as P

D = 1280
HD = 64
EPS = 1e-06
F32 = jnp.float32
BF16 = jnp.bfloat16
Z = ("zh", "zl")
BLOCK = 256
LOG2E = 1.4426950408889634


def ring(count, step):
    return [(i, (i + step) % count) for i in range(count)]


def shift(block, axis, count, step):
    return lax.ppermute(block, axis, ring(count, step))


def swap_core(block):
    return lax.ppermute(block, "co", [(0, 1), (1, 0)])


RING_ORDER = (0, 7, 1, 6, 2, 5, 3, 4)


def four_blocks(block, axis):
    return [block] + [shift(block, axis, 4, 4 - away) for away in (1, 2, 3)]


def in_order(blocks, me):
    slots = []
    for slot in range(4):
        away = (slot + 4 - me) % 4
        pick = jnp.where(away == 0, blocks[0], blocks[1])
        pick = jnp.where(away == 2, blocks[2], pick)
        slots.append(jnp.where(away == 3, blocks[3], pick))
    return jnp.concatenate(slots, axis=0)


def ring_z(block):
    ahead = behind = block
    blocks = [block]
    for step in range(1, 5):
        ahead = shift(ahead, Z, 8, 1)
        blocks.append(ahead)
        if step < 4:
            behind = shift(behind, Z, 8, -1)
            blocks.append(behind)
    return jnp.stack(blocks)


def chunk_squares(read, count, width):
    def step(index, total):
        wide = read(index).astype(F32)
        return total + jnp.sum((wide * wide).reshape(-1, 8, width), axis=0)

    return jnp.sum(lax.fori_loop(0, count, step, jnp.zeros((8, width), F32)), axis=0, keepdims=True)


def attention_kernel(start_ref, q_ref, before_ref, own_ref, o_ref):
    heads = q_ref.shape[0] // HD

    def window(kind, head, block):
        rows = pl.ds(pl.multiple_of((kind * heads + head) * HD, HD), HD)
        ref, block = (before_ref, block) if block < 2 else (own_ref, block - 2)
        return ref[rows, block * BLOCK : (block + 1) * BLOCK]

    key_row = lax.broadcasted_iota(jnp.int32, (BLOCK, BLOCK), 0)
    query_col = lax.broadcasted_iota(jnp.int32, (BLOCK, BLOCK), 1)
    causal = key_row <= query_col

    def one_head(head, carry):
        rows = pl.ds(pl.multiple_of(head * HD, HD), HD)
        for part in range(q_ref.shape[1] // BLOCK):
            cols = slice(part * BLOCK, (part + 1) * BLOCK)
            query = q_ref[rows, cols]
            start = start_ref[:, cols]
            scores = []
            for step in range(3):
                base = (part + step) * BLOCK
                keys = window(0, head, part + step)
                score = lax.dot_general(
                    keys, query, (((0,), (0,)), ((), ())), preferred_element_type=F32
                )
                allowed = key_row >= start - base
                if step == 2:
                    allowed = allowed & causal
                scores.append(jnp.where(allowed, score, -1e30))
            top = jnp.maximum(jnp.maximum(scores[0], scores[1]), scores[2])
            top = jnp.max(top, axis=0, keepdims=True)
            total = jnp.zeros((1, BLOCK), F32)
            mixed = jnp.zeros((HD, BLOCK), F32)
            for step in range(3):
                weight = jnp.exp2((scores[step] - top) * (math.sqrt(HD) * LOG2E))
                total = total + jnp.sum(weight, axis=0, keepdims=True)
                mixed = mixed + jnp.dot(
                    window(1, head, part + step),
                    weight.astype(BF16),
                    preferred_element_type=F32,
                )
            o_ref[rows, cols] = (mixed / total).astype(BF16)
        return carry

    lax.fori_loop(0, heads, one_head, 0)


def attention(start, query, before, own):
    return pl.pallas_call(
        attention_kernel,
        out_shape=jax.ShapeDtypeStruct(query.shape, BF16),
        in_specs=[pl.BlockSpec(memory_space=pltpu.VMEM)] * 4,
        out_specs=pl.BlockSpec(memory_space=pltpu.VMEM),
        cost_estimate=pl.CostEstimate(flops=800_000_000, bytes_accessed=4_000_000, transcendentals=3_000_000),
        name="attention",
    )(start, query, before, own)


def stream_starts(segment):
    order = jnp.arange(segment.shape[0], dtype=jnp.int32)
    earlier = jnp.concatenate([segment[:1], segment[:-1]])
    return lax.cummax(jnp.where(segment != earlier, order, jnp.zeros_like(order)))


def project_kernel(
    place_ref, x0_ref, x1_ref, x2_ref, x3_ref, near_ref, far_ref, gain_ref, cos_ref, sin_ref,
    query_ref, own_ref, features_ref, size_ref, held, weight, result,
):
    tp, core, ring = place_ref[0], place_ref[1], place_ref[2]
    for away, ref in enumerate((x0_ref, x1_ref, x2_ref, x3_ref)):
        block = (tp + away) % 4
        held[0, block] = ref[:160]
        held[1, block] = ref[160:]
    for slot, away in enumerate(RING_ORDER):
        weight[core, (ring + away) % 8] = near_ref[slot]
        weight[1 - core, (ring + away) % 8] = far_ref[slot]
    rows = query_ref.shape[1]
    local = query_ref.shape[0]
    tokens = held[...].reshape(D, rows)
    features_ref[...] = tokens
    size = lax.rsqrt(
        chunk_squares(lambda i: features_ref[pl.ds(pl.multiple_of(i * 160, 160), 160), :], 8, rows) + EPS
    )
    size_ref[...] = size
    for kind in range(3):
        part = weight[:, :, :, kind * local : (kind + 1) * local].reshape(D, local)
        turned = jnp.transpose(part)
        wide = turned.astype(F32)
        length = lax.rsqrt(jnp.sum(wide * wide, axis=1, keepdims=True) + EPS)
        raw = jnp.dot(turned, features_ref[...], preferred_element_type=F32)
        result[kind * local : (kind + 1) * local] = raw * length * size
    half = HD // 2
    cosine, sine = cos_ref[...], sin_ref[...]

    def one_head(index, carry):
        span = pl.ds(pl.multiple_of(index * HD, HD), HD)
        gain = gain_ref[span, :]
        for kind, target in ((0, query_ref), (1, own_ref)):
            part = result[pl.ds(pl.multiple_of(kind * local + index * HD, HD), HD), :]
            length = lax.rsqrt(jnp.sum(part * part, axis=0, keepdims=True) + EPS)
            part = (gain * (part * length)).astype(BF16).astype(F32)
            first, second = part[:half], part[half:]
            both = [first * cosine - second * sine, first * sine + second * cosine]
            target[span, :] = jnp.concatenate(both, axis=0).astype(BF16)
        spot = pl.ds(pl.multiple_of(local + index * HD, HD), HD)
        own_ref[spot, :] = result[pl.ds(pl.multiple_of(2 * local + index * HD, HD), HD), :].astype(BF16)
        return carry

    lax.fori_loop(0, local // HD, one_head, 0)


SMALL = pl.BlockSpec(memory_space=pltpu.SMEM)
NEAR = pl.BlockSpec(memory_space=pltpu.VMEM)
FAR = pl.BlockSpec(memory_space=pl.ANY)


def project(spot, blocks, near, far, gain, cosine, sine):
    local, rows = blocks[0].shape
    return pl.pallas_call(
        project_kernel,
        out_shape=[
            jax.ShapeDtypeStruct((local, rows), BF16),
            jax.ShapeDtypeStruct((2 * local, rows), BF16),
            jax.ShapeDtypeStruct((D, rows), BF16),
            jax.ShapeDtypeStruct((1, rows), F32),
        ],
        in_specs=[SMALL] + [NEAR] * 9,
        out_specs=[NEAR] * 4,
        scratch_shapes=[
            pltpu.VMEM((2, 4, 160, rows), BF16),
            pltpu.VMEM((2, 8, 80, 3 * local), BF16),
            pltpu.VMEM((3 * local, rows), F32),
        ],
        compiler_params=pltpu.CompilerParams(vmem_limit_bytes=40 * 2**20),
        cost_estimate=pl.CostEstimate(flops=1_900_000_000, bytes_accessed=12_000_000, transcendentals=0),
        name="project",
    )(spot, *blocks, near, far, gain, cosine, sine)


def layer_kernel(
    place_ref, a0_ref, a1_ref, a2_ref, a3_ref, features_ref, size_ref, attn_ref,
    up_ref, gate_ref, near_ref, far_ref, wide_near_ref, wide_far_ref,
    part_ref, mixed_ref, attended, state, turned, inner, narrow, wide, sems,
):
    tp, core, ring = place_ref[0], place_ref[1], place_ref[2]
    rows = features_ref.shape[1]
    hidden = up_ref.shape[1]
    copies = []
    for slot, away in enumerate(RING_ORDER):
        spot = (ring + away) % 8
        copies.append(pltpu.make_async_copy(near_ref.at[slot], narrow.at[core, spot], sems.at[slot]))
        copies.append(pltpu.make_async_copy(far_ref.at[slot], narrow.at[1 - core, spot], sems.at[8 + slot]))
    late = [
        pltpu.make_async_copy(wide_near_ref, wide.at[core], sems.at[16]),
        pltpu.make_async_copy(wide_far_ref, wide.at[1 - core], sems.at[17]),
    ]
    for copy in copies + late:
        copy.start()
    for away, ref in enumerate((a0_ref, a1_ref, a2_ref, a3_ref)):
        attended[away * 320 : (away + 1) * 320] = ref[...]
    for copy in copies:
        copy.wait()

    def out_rows(index, cols):
        return narrow[index // 4, pl.ds(2 * (index % 4), 2), :, cols].reshape(160, -1)

    out_length = lax.rsqrt(chunk_squares(lambda i: out_rows(i, slice(0, D)), 8, D) + EPS)

    def project_out(index, total):
        upper = (out_rows(2 * index, slice(0, D)).astype(F32) * out_length).astype(BF16)
        lower = (out_rows(2 * index + 1, slice(0, D)).astype(F32) * out_length).astype(BF16)
        block = jnp.dot(
            jnp.concatenate([upper, lower], axis=0), attended[...], preferred_element_type=F32
        )
        state[pl.ds(pl.multiple_of(index * 320, 320), 320), :] = block
        return total + jnp.sum((block * block).reshape(-1, 8, rows), axis=0)

    zero = jnp.zeros((8, rows), F32)
    total = jnp.sum(lax.fori_loop(0, 4, project_out, zero), axis=0, keepdims=True)
    pull = lax.rsqrt(total + EPS)
    size = size_ref[...]

    def mix(index, total):
        span = pl.ds(pl.multiple_of(index * 128, 128), 128)
        before = features_ref[span, :].astype(F32) * size
        mixed = before + attn_ref[span, :] * (state[span, :] * pull - before)
        state[span, :] = mixed
        return total + jnp.sum((mixed * mixed).reshape(-1, 8, rows), axis=0)

    total = jnp.sum(lax.fori_loop(0, D // 128, mix, zero), axis=0, keepdims=True)
    scale = lax.rsqrt(total + EPS)

    def turn(index, carry):
        span = pl.ds(pl.multiple_of(index * 128, 128), 128)
        mixed = state[span, :] * scale
        state[span, :] = mixed
        turned[:, span] = jnp.transpose(mixed).astype(BF16)
        return carry

    lax.fori_loop(0, D // 128, turn, 0)
    for other in range(2):
        spot = pl.ds(pl.multiple_of(other * 640 + tp * 160, 160), 160)
        mixed_ref[other * 160 : (other + 1) * 160] = state[spot, :]
    for copy in late:
        copy.wait()

    def column_length(ref, cols):
        weight = ref[..., cols].reshape(D, BLOCK).astype(F32)
        return lax.rsqrt(jnp.sum(weight * weight, axis=0, keepdims=True) + EPS)

    def expand(index, carry):
        cols = pl.ds(pl.multiple_of(index * BLOCK, BLOCK), BLOCK)
        gate_cols = pl.ds(pl.multiple_of(hidden + index * BLOCK, BLOCK), BLOCK)
        up = jnp.dot(turned[...], wide[:, :, cols].reshape(D, BLOCK), preferred_element_type=F32)
        gate = jnp.dot(turned[...], wide[:, :, gate_cols].reshape(D, BLOCK), preferred_element_type=F32)
        down = column_length(narrow, pl.ds(pl.multiple_of(D + index * BLOCK, BLOCK), BLOCK))
        up = up * (up_ref[:, cols] * column_length(wide, cols) * down)
        gate = gate * (gate_ref[:, cols] * column_length(wide, gate_cols) * math.sqrt(D))
        inner[:, cols] = (up * (gate / (1.0 + jnp.exp(-gate)))).astype(BF16)
        return carry

    lax.fori_loop(0, hidden // BLOCK, expand, 0)
    columns = slice(D, D + hidden)

    def contract(index, carry):
        left = jnp.concatenate(
            [out_rows(2 * index, columns), out_rows(2 * index + 1, columns)], axis=0
        )
        block = lax.dot_general(
            left, inner[...], (((1,), (1,)), ((), ())), preferred_element_type=F32
        ).astype(BF16)
        other, first = index // 2, 2 * (index % 2)
        span = pl.ds(pl.multiple_of(other * 160, 160), 160)
        part_ref[first, span, :] = block[:160]
        part_ref[first + 1, span, :] = block[160:]
        return carry

    lax.fori_loop(0, 4, contract, 0)


def layer(spot, attended, features, size, attn_step, up_scale, gate_scale, near, far, wide_near, wide_far):
    local, rows = attended[0].shape
    hidden = up_scale.shape[1]
    return pl.pallas_call(
        layer_kernel,
        out_shape=[
            jax.ShapeDtypeStruct((4, local, rows), BF16),
            jax.ShapeDtypeStruct((local, rows), F32),
        ],
        in_specs=[SMALL] + [NEAR] * 9 + [FAR] * 4,
        out_specs=[NEAR] * 2,
        scratch_shapes=[
            pltpu.VMEM((D, rows), BF16),
            pltpu.VMEM((D, rows), F32),
            pltpu.VMEM((rows, D), BF16),
            pltpu.VMEM((rows, hidden), BF16),
            pltpu.VMEM((2, 8, 80, 2 * hidden), BF16),
            pltpu.VMEM((2, 640, 2 * hidden), BF16),
            pltpu.SemaphoreType.DMA((18,)),
        ],
        compiler_params=pltpu.CompilerParams(vmem_limit_bytes=56 * 2**20),
        cost_estimate=pl.CostEstimate(flops=10_000_000_000, bytes_accessed=20_000_000, transcendentals=1_000_000),
        name="layer",
    )(spot, *attended, features, size, attn_step, up_scale, gate_scale, near, far, wide_near, wide_far)


def feature_order(array):
    parts = array.reshape(4, 4, 2, 2, 20)
    return parts.transpose(3, 0, 2, 1, 4).reshape(D, 1)


def body(
    tokens,
    qkv_weight,
    out_weight,
    gate_up_weight,
    down_weight,
    qk_scale,
    attn_rate,
    mlp_rate,
    up_scale,
    gate_scale,
    segment_ids,
):
    rows = tokens.shape[1]
    local = tokens.shape[2]
    hidden = gate_up_weight.shape[2]
    tp = lax.axis_index("tp")
    core = lax.axis_index("co")
    spot_y = lax.axis_index("y")
    spot_z = lax.axis_index("zh") * 2 + lax.axis_index("zl")
    piece = lax.axis_index("zl") * 2 + core
    spot = jnp.stack([tp, core, spot_z]).astype(jnp.int32)

    qkv = qkv_weight.astype(BF16).reshape(20, 3 * local)
    qkv_near = ring_z(in_order(four_blocks(qkv, "y"), spot_y))
    qkv_far = swap_core(qkv_near)

    own_tokens = tokens[0].T.reshape(4, 2, 2, 20, rows).transpose(2, 1, 0, 3, 4).reshape(local, rows)
    blocks = four_blocks(own_tokens, "tp")

    wide = gate_up_weight.astype(BF16).reshape(20, 2 * hidden)
    wide = lax.all_gather(lax.all_gather(wide, Z), "y")
    wide_near = wide.transpose(1, 0, 2, 3).reshape(640, 2 * hidden)
    wide_far = swap_core(wide_near)

    out_rows = jnp.concatenate(four_blocks(out_weight.T.astype(BF16), "tp"), axis=1)
    narrow = jnp.concatenate([out_rows, down_weight.T.astype(BF16)], axis=1)
    narrow_near = ring_z(in_order(four_blocks(narrow, "y"), spot_y))
    narrow_far = swap_core(narrow_near)

    starts = stream_starts(segment_ids[0])
    own_first = piece * rows
    own_start = lax.dynamic_slice_in_dim(starts, own_first, rows)
    position = own_first + jnp.arange(rows, dtype=jnp.int32) - own_start
    frequency = jnp.exp(-math.log(10000.0) * jnp.arange(HD // 2, dtype=F32) * 2.0 / HD)
    angles = frequency[:, None] * position.astype(F32)[None]
    query, own, features, size = project(
        spot, blocks, qkv_near, qkv_far, qk_scale[:, None], jnp.cos(angles), jnp.sin(angles)
    )
    window = 2 * BLOCK
    before = lax.ppermute(own[:, rows - window :], ("zl", "co"), [(i, i + 1) for i in range(3)])
    attended = attention((own_start - own_first + window)[None], query, before, own)

    parts, mixed = layer(
        spot,
        four_blocks(attended, "tp"),
        features,
        size,
        feature_order(attn_rate),
        up_scale[None],
        gate_scale[None],
        narrow_near,
        narrow_far,
        wide_near,
        wide_far,
    )
    mlp_block = lax.dynamic_index_in_dim(parts, tp, 0, keepdims=False).astype(F32)
    for step in (2, 1, 3):
        sent = lax.dynamic_index_in_dim(parts, (tp + step) % 4, 0, keepdims=False)
        mlp_block = mlp_block + shift(sent, "tp", 4, step).astype(F32)

    steps = feature_order(mlp_rate).reshape(2, 4, 160)
    step_block = lax.dynamic_index_in_dim(steps, tp, 1, keepdims=False).reshape(local, 1)
    kept = mixed - step_block * mixed
    moved = step_block * mlp_block
    sums = jnp.stack(
        [
            jnp.sum(mlp_block * mlp_block, axis=0),
            jnp.sum(kept * kept, axis=0),
            jnp.sum(kept * moved, axis=0),
            jnp.sum(moved * moved, axis=0),
        ]
    )
    sums = sum(four_blocks(sums, "tp"))
    pull = lax.rsqrt(sums[0] + EPS)
    length = jnp.maximum(sums[1] + 2.0 * pull * sums[2] + pull * pull * sums[3], 0.0)
    final = math.sqrt(D) * lax.rsqrt(length + EPS)
    result = ((kept + pull[None] * moved) * final[None]).astype(BF16)
    result = result.reshape(2, 2, 4, 20, rows).transpose(2, 1, 0, 3, 4).reshape(local, rows)
    return result.T[None]


def solution(mesh):
    fine = Mesh(mesh.devices.reshape(4, 4, 4, 2, 2), ("zh", "y", "tp", "zl", "co"))
    rep, cp = ("zh", "y"), ("zl", "co")
    in_specs = (
        P(rep, cp, "tp"),
        P(rep + cp, None, "tp"),
        P("tp", rep + cp),
        P(rep + cp, None, "tp"),
        P("tp", rep + cp),
        P("tp"),
        P(),
        P(),
        P("tp"),
        P("tp"),
        P(rep, None),
    )
    return jax.shard_map(
        body, mesh=fine, in_specs=in_specs, out_specs=P(rep, cp, "tp"), check_vma=False
    )
```

```python
import math

import jax
import jax.numpy as jnp
from jax import lax
from jax.experimental import pallas as pl
from jax.experimental.pallas import tpu as pltpu
from jax.sharding import Mesh, PartitionSpec as P

D = 1280
HD = 64
EPS = 1e-06
F32 = jnp.float32
BF16 = jnp.bfloat16
Z = ("zh", "zl")
BLOCK = 256
LOG2E = 1.4426950408889634


def ring(count, step):
    return [(i, (i + step) % count) for i in range(count)]


def shift(block, axis, count, step):
    return lax.ppermute(block, axis, ring(count, step))


def swap_core(block):
    return lax.ppermute(block, "co", [(0, 1), (1, 0)])


SHARDS = 64
SHARD = 20
PADDED = 24
WIDE = SHARDS * PADDED
GROUP = 16 * PADDED
SMALL = pl.BlockSpec(memory_space=pltpu.SMEM)
NEAR = pl.BlockSpec(memory_space=pltpu.VMEM)
FAR = pl.BlockSpec(memory_space=pl.ANY)


def four_blocks(block, axis):
    return [block] + [shift(block, axis, 4, 4 - away) for away in (1, 2, 3)]


def after(blocks, *earlier):
    return list(lax.optimization_barrier((tuple(blocks), earlier))[0])


def strip(block):
    shards = [block[shard * PADDED : shard * PADDED + SHARD] for shard in range(16)]
    return jnp.concatenate(shards, axis=0)


def chunk_squares(read, count, width):
    def step(index, total):
        wide = read(index).astype(F32)
        return total + jnp.sum((wide * wide).reshape(-1, 8, width), axis=0)

    return jnp.sum(lax.fori_loop(0, count, step, jnp.zeros((8, width), F32)), axis=0, keepdims=True)


def attention_kernel(start_ref, q_ref, before_ref, own_ref, o_ref):
    heads = q_ref.shape[0] // HD

    def window(kind, head, block):
        rows = pl.ds(pl.multiple_of((kind * heads + head) * HD, HD), HD)
        ref, block = (before_ref, block) if block < 2 else (own_ref, block - 2)
        return ref[rows, block * BLOCK : (block + 1) * BLOCK]

    key_row = lax.broadcasted_iota(jnp.int32, (BLOCK, BLOCK), 0)
    query_col = lax.broadcasted_iota(jnp.int32, (BLOCK, BLOCK), 1)
    causal = key_row <= query_col

    def one_head(head, carry):
        rows = pl.ds(pl.multiple_of(head * HD, HD), HD)
        for part in range(q_ref.shape[1] // BLOCK):
            cols = slice(part * BLOCK, (part + 1) * BLOCK)
            query = q_ref[rows, cols]
            start = start_ref[:, cols]
            scores = []
            for step in range(3):
                base = (part + step) * BLOCK
                keys = window(0, head, part + step)
                score = lax.dot_general(
                    keys, query, (((0,), (0,)), ((), ())), preferred_element_type=F32
                )
                allowed = key_row >= start - base
                if step == 2:
                    allowed = allowed & causal
                scores.append(jnp.where(allowed, score, -1e30))
            top = jnp.maximum(jnp.maximum(scores[0], scores[1]), scores[2])
            top = jnp.max(top, axis=0, keepdims=True)
            total = jnp.zeros((1, BLOCK), F32)
            mixed = jnp.zeros((HD, BLOCK), F32)
            for step in range(3):
                weight = jnp.exp2((scores[step] - top) * (math.sqrt(HD) * LOG2E))
                total = total + jnp.sum(weight, axis=0, keepdims=True)
                mixed = mixed + jnp.dot(
                    window(1, head, part + step),
                    weight.astype(BF16),
                    preferred_element_type=F32,
                )
            o_ref[rows, cols] = (mixed / total).astype(BF16)
        return carry

    lax.fori_loop(0, heads, one_head, 0)


def attention(start, query, before, own):
    return pl.pallas_call(
        attention_kernel,
        out_shape=jax.ShapeDtypeStruct(query.shape, BF16),
        in_specs=[pl.BlockSpec(memory_space=pltpu.VMEM)] * 4,
        out_specs=pl.BlockSpec(memory_space=pltpu.VMEM),
        cost_estimate=pl.CostEstimate(flops=800_000_000, bytes_accessed=4_000_000, transcendentals=3_000_000),
        name="attention",
    )(start, query, before, own)


def stream_starts(segment):
    order = jnp.arange(segment.shape[0], dtype=jnp.int32)
    earlier = jnp.concatenate([segment[:1], segment[:-1]])
    return lax.cummax(jnp.where(segment != earlier, order, jnp.zeros_like(order)))


def project_kernel(
    place_ref, x0_ref, x1_ref, x2_ref, x3_ref, w0_ref, w1_ref, w2_ref, w3_ref, far_ref, gain_ref, cos_ref, sin_ref,
    query_ref, own_ref, features_ref, size_ref, held, weight, result,
):
    tp, core, spot_y = place_ref[0], place_ref[1], place_ref[2]
    rows = query_ref.shape[1]
    local = query_ref.shape[0]
    held[...] = jnp.zeros_like(held)
    for away, ref in enumerate((x0_ref, x1_ref, x2_ref, x3_ref)):
        for shard in range(16):
            held[(tp + away) % 4, shard, :SHARD] = ref[shard * SHARD : (shard + 1) * SHARD]
    for away, ref in enumerate((w0_ref, w1_ref, w2_ref, w3_ref)):
        y = (spot_y + away) % 4
        for z in range(8):
            weight[z // 2, y, z % 2, core] = ref[z]
            weight[z // 2, y, z % 2, 1 - core] = far_ref[away, z]
    features_ref[...] = held[...].reshape(WIDE, rows)
    size = lax.rsqrt(
        chunk_squares(lambda i: features_ref[pl.ds(pl.multiple_of(i * 128, 128), 128), :], WIDE // 128, rows) + EPS
    )
    size_ref[...] = size
    for kind in range(3):
        part = weight[..., kind * local : (kind + 1) * local].reshape(WIDE, local)
        turned = jnp.transpose(part)
        wide = turned.astype(F32)
        length = lax.rsqrt(jnp.sum(wide * wide, axis=1, keepdims=True) + EPS)
        raw = jnp.dot(turned, features_ref[...], preferred_element_type=F32)
        result[kind * local : (kind + 1) * local] = raw * length * size
    half = HD // 2
    cosine, sine = cos_ref[...], sin_ref[...]

    def one_head(index, carry):
        span = pl.ds(pl.multiple_of(index * HD, HD), HD)
        gain = gain_ref[span, :]
        for kind, target in ((0, query_ref), (1, own_ref)):
            part = result[pl.ds(pl.multiple_of(kind * local + index * HD, HD), HD), :]
            length = lax.rsqrt(jnp.sum(part * part, axis=0, keepdims=True) + EPS)
            part = (gain * (part * length)).astype(BF16).astype(F32)
            first, second = part[:half], part[half:]
            both = [first * cosine - second * sine, first * sine + second * cosine]
            target[span, :] = jnp.concatenate(both, axis=0).astype(BF16)
        spot = pl.ds(pl.multiple_of(local + index * HD, HD), HD)
        own_ref[spot, :] = result[pl.ds(pl.multiple_of(2 * local + index * HD, HD), HD), :].astype(BF16)
        return carry

    lax.fori_loop(0, local // HD, one_head, 0)


def project(spot, blocks, near, far, gain, cosine, sine):
    local, rows = blocks[0].shape
    return pl.pallas_call(
        project_kernel,
        out_shape=[
            jax.ShapeDtypeStruct((local, rows), BF16),
            jax.ShapeDtypeStruct((2 * local, rows), BF16),
            jax.ShapeDtypeStruct((WIDE, rows), BF16),
            jax.ShapeDtypeStruct((1, rows), F32),
        ],
        in_specs=[SMALL] + [NEAR] * 12,
        out_specs=[NEAR] * 4,
        scratch_shapes=[
            pltpu.VMEM((4, 16, PADDED, rows), BF16),
            pltpu.VMEM((4, 4, 2, 2, PADDED, 3 * local), BF16),
            pltpu.VMEM((3 * local, rows), F32),
        ],
        compiler_params=pltpu.CompilerParams(vmem_limit_bytes=40 * 2**20),
        cost_estimate=pl.CostEstimate(flops=1_900_000_000, bytes_accessed=12_000_000, transcendentals=0),
        name="project",
    )(spot, *blocks, *near, far, gain, cosine, sine)


def layer_kernel(
    place_ref, a0_ref, a1_ref, a2_ref, a3_ref, features_ref, size_ref, attn_ref, up_ref, gate_ref, weight_ref,
    part_ref, mixed_ref, attended, state, turned, inner, weight, sems,
):
    tp = place_ref[0]
    rows = features_ref.shape[1]
    hidden = up_ref.shape[1]
    bounds = (0, D, D + 2 * hidden, D + 3 * hidden)
    copies = []
    for kind in range(3):
        cols = slice(bounds[kind], bounds[kind + 1])
        copies.append(pltpu.make_async_copy(weight_ref.at[:, :, cols], weight.at[:, :, cols], sems.at[kind]))
        copies[kind].start()
    for away, ref in enumerate((a0_ref, a1_ref, a2_ref, a3_ref)):
        attended[away * 320 : (away + 1) * 320] = ref[...]
    copies[0].wait()

    def group(index, cols):
        return weight[pl.ds(16 * index, 16), :, cols].reshape(GROUP, -1)

    def eighth(index):
        return weight[pl.ds(8 * index, 8), :, :D].reshape(8 * PADDED, D)

    out_length = lax.rsqrt(chunk_squares(eighth, 8, D) + EPS)

    def project_out(index, total):
        left = (group(index, slice(0, D)).astype(F32) * out_length).astype(BF16)
        block = jnp.dot(left, attended[...], preferred_element_type=F32)
        state[pl.ds(pl.multiple_of(index * GROUP, GROUP), GROUP), :] = block
        return total + jnp.sum((block * block).reshape(-1, 8, rows), axis=0)

    zero = jnp.zeros((8, rows), F32)
    total = jnp.sum(lax.fori_loop(0, 4, project_out, zero), axis=0, keepdims=True)
    pull = lax.rsqrt(total + EPS)
    size = size_ref[...]

    def mix(index, total):
        span = pl.ds(pl.multiple_of(index * 128, 128), 128)
        before = features_ref[span, :].astype(F32) * size
        mixed = before + attn_ref[span, :] * (state[span, :] * pull - before)
        state[span, :] = mixed
        return total + jnp.sum((mixed * mixed).reshape(-1, 8, rows), axis=0)

    total = jnp.sum(lax.fori_loop(0, WIDE // 128, mix, zero), axis=0, keepdims=True)
    scale = lax.rsqrt(total + EPS)

    def turn(index, carry):
        span = pl.ds(pl.multiple_of(index * 128, 128), 128)
        mixed = state[span, :] * scale
        state[span, :] = mixed
        turned[:, span] = jnp.transpose(mixed).astype(BF16)
        return carry

    lax.fori_loop(0, WIDE // 128, turn, 0)
    mixed_ref[...] = strip(state[pl.ds(pl.multiple_of(tp * GROUP, GROUP), GROUP), :])
    copies[1].wait()
    copies[2].wait()

    def columns(start, index):
        return weight[:, :, pl.ds(pl.multiple_of(start + index * BLOCK, BLOCK), BLOCK)].reshape(WIDE, BLOCK)

    def length(part):
        wide = part.astype(F32)
        return lax.rsqrt(jnp.sum(wide * wide, axis=0, keepdims=True) + EPS)

    def expand(index, carry):
        cols = pl.ds(pl.multiple_of(index * BLOCK, BLOCK), BLOCK)
        up_part, gate_part = columns(D, index), columns(D + hidden, index)
        up = jnp.dot(turned[...], up_part, preferred_element_type=F32)
        gate = jnp.dot(turned[...], gate_part, preferred_element_type=F32)
        up = up * (up_ref[:, cols] * length(up_part) * length(columns(D + 2 * hidden, index)))
        gate = gate * (gate_ref[:, cols] * length(gate_part) * math.sqrt(D))
        inner[:, cols] = (up * (gate / (1.0 + jnp.exp(-gate)))).astype(BF16)
        return carry

    lax.fori_loop(0, hidden // BLOCK, expand, 0)

    def contract(index, carry):
        block = lax.dot_general(
            group(index, slice(D + 2 * hidden, D + 3 * hidden)),
            inner[...],
            (((1,), (1,)), ((), ())),
            preferred_element_type=F32,
        )
        part_ref[index] = strip(block).astype(BF16)
        return carry

    lax.fori_loop(0, 4, contract, 0)


def layer(spot, attended, features, size, attn_step, up_scale, gate_scale, weight):
    local, rows = attended[0].shape
    hidden = up_scale.shape[1]
    return pl.pallas_call(
        layer_kernel,
        out_shape=[
            jax.ShapeDtypeStruct((4, local, rows), BF16),
            jax.ShapeDtypeStruct((local, rows), F32),
        ],
        in_specs=[SMALL] + [NEAR] * 9 + [FAR],
        out_specs=[NEAR] * 2,
        scratch_shapes=[
            pltpu.VMEM((D, rows), BF16),
            pltpu.VMEM((WIDE, rows), F32),
            pltpu.VMEM((rows, WIDE), BF16),
            pltpu.VMEM((rows, hidden), BF16),
            pltpu.VMEM((SHARDS, PADDED, D + 3 * hidden), BF16),
            pltpu.SemaphoreType.DMA((3,)),
        ],
        compiler_params=pltpu.CompilerParams(vmem_limit_bytes=56 * 2**20),
        cost_estimate=pl.CostEstimate(flops=10_000_000_000, bytes_accessed=20_000_000, transcendentals=1_000_000),
        name="layer",
    )(spot, *attended, features, size, attn_step, up_scale, gate_scale, weight)


def body(
    tokens,
    qkv_weight,
    out_weight,
    gate_up_weight,
    down_weight,
    qk_scale,
    attn_rate,
    mlp_rate,
    up_scale,
    gate_scale,
    segment_ids,
):
    rows = tokens.shape[1]
    local = tokens.shape[2]
    hidden = gate_up_weight.shape[2]
    tp = lax.axis_index("tp")
    core = lax.axis_index("co")
    spot_y = lax.axis_index("y")
    piece = lax.axis_index("zl") * 2 + core
    spot = jnp.stack([tp, core, spot_y]).astype(jnp.int32)

    def pad(shard):
        return jnp.pad(shard, ((0, PADDED - SHARD), (0, 0)))

    out_rows = four_blocks(out_weight.T.astype(BF16), "tp")
    wide = gate_up_weight.astype(BF16).reshape(SHARD, 2 * hidden)
    rest = pad(jnp.concatenate(out_rows + [wide, down_weight.T.astype(BF16)], axis=1))
    weight = lax.all_gather(rest, ("zh", "y", "zl", "co"))

    own_tokens, qkv = after([tokens[0].T, pad(qkv_weight.astype(BF16).reshape(SHARD, 3 * local))], rest)
    blocks = four_blocks(own_tokens, "tp")
    everywhere = jnp.broadcast_to(qkv[None], (8,) + qkv.shape)
    qkv_z = lax.all_to_all(everywhere, Z, 0, 0, tiled=True)
    (qkv_z,) = after([qkv_z], *blocks)
    qkv_near = four_blocks(qkv_z, "y")
    qkv_far = swap_core(jnp.stack(qkv_near))

    starts = stream_starts(segment_ids[0])
    own_first = piece * rows
    own_start = lax.dynamic_slice_in_dim(starts, own_first, rows)
    position = own_first + jnp.arange(rows, dtype=jnp.int32) - own_start
    frequency = jnp.exp(-math.log(10000.0) * jnp.arange(HD // 2, dtype=F32) * 2.0 / HD)
    angles = frequency[:, None] * position.astype(F32)[None]
    query, own, features, size = project(
        spot, blocks, qkv_near, qkv_far, qk_scale[:, None], jnp.cos(angles), jnp.sin(angles)
    )
    window = 2 * BLOCK
    before = lax.ppermute(own[:, rows - window :], ("zl", "co"), [(i, i + 1) for i in range(3)])
    attended = attention((own_start - own_first + window)[None], query, before, own)

    parts, mixed = layer(
        spot,
        four_blocks(attended, "tp"),
        features,
        size,
        jnp.pad(attn_rate.reshape(SHARDS, SHARD), ((0, 0), (0, PADDED - SHARD))).reshape(WIDE, 1),
        up_scale[None],
        gate_scale[None],
        weight,
    )
    landed = lax.all_to_all(parts, "tp", 0, 0, tiled=True).astype(F32)
    mlp_block = landed[0] + landed[1] + landed[2] + landed[3]

    step_block = lax.dynamic_slice_in_dim(mlp_rate, tp * local, local)[:, None]
    kept = mixed - step_block * mixed
    moved = step_block * mlp_block
    sums = jnp.stack(
        [
            jnp.sum(mlp_block * mlp_block, axis=0),
            jnp.sum(kept * kept, axis=0),
            jnp.sum(kept * moved, axis=0),
            jnp.sum(moved * moved, axis=0),
        ]
    )
    sums = sum(four_blocks(sums, "tp"))
    pull = lax.rsqrt(sums[0] + EPS)
    length = jnp.maximum(sums[1] + 2.0 * pull * sums[2] + pull * pull * sums[3], 0.0)
    final = math.sqrt(D) * lax.rsqrt(length + EPS)
    result = ((kept + pull[None] * moved) * final[None]).astype(BF16)
    return result.T[None]


def solution(mesh):
    fine = Mesh(mesh.devices.reshape(4, 4, 4, 2, 2), ("zh", "y", "tp", "zl", "co"))
    rep, cp = ("zh", "y"), ("zl", "co")
    in_specs = (
        P(rep, cp, "tp"),
        P(rep + cp, None, "tp"),
        P("tp", rep + cp),
        P(rep + cp, None, "tp"),
        P("tp", rep + cp),
        P("tp"),
        P(),
        P(),
        P("tp"),
        P("tp"),
        P(rep, None),
    )
    return jax.shard_map(
        body, mesh=fine, in_specs=in_specs, out_specs=P(rep, cp, "tp"), check_vma=False
    )
```

```python
import functools
import math

import jax
import jax.numpy as jnp
from jax import lax
from jax.experimental import pallas as pl
from jax.experimental.pallas import tpu as pltpu
from jax.sharding import Mesh, PartitionSpec as P

D = 1280
HD = 64
EPS = 1e-06
F32 = jnp.float32
BF16 = jnp.bfloat16
Z = ("zh", "zl")
BLOCK = 256
LOG2E = 1.4426950408889634


def ring(count, step):
    return [(i, (i + step) % count) for i in range(count)]


def shift(block, axis, count, step):
    return lax.ppermute(block, axis, ring(count, step))


def swap_core(block):
    return lax.ppermute(block, "co", [(0, 1), (1, 0)])


SHARD = 20
RING_ORDER = (0, 7, 1, 6, 2, 5, 3, 4)
SMALL = pl.BlockSpec(memory_space=pltpu.SMEM)
NEAR = pl.BlockSpec(memory_space=pltpu.VMEM)
FAR = pl.BlockSpec(memory_space=pl.ANY)


def four_blocks(block, axis):
    return [block] + [shift(block, axis, 4, 4 - away) for away in (1, 2, 3)]


def after(blocks, *earlier):
    return list(lax.optimization_barrier((tuple(blocks), earlier))[0])


def order_kernel(which, aways, place_ref, *refs):
    count = len(aways)
    blocks, whole_ref, held = refs[:count], refs[count], refs[count + 1]
    me = place_ref[which]
    for block, away in zip(blocks, aways):
        held[(me + away) % count] = block[...]
    whole_ref[...] = jnp.concatenate([held[slot] for slot in range(count)], axis=0)


def in_order(spot, which, blocks, aways):
    rows, cols = blocks[0].shape
    count = len(blocks)
    return pl.pallas_call(
        functools.partial(order_kernel, which, aways),
        out_shape=jax.ShapeDtypeStruct((count * rows, cols), BF16),
        in_specs=[SMALL] + [NEAR] * count,
        out_specs=NEAR,
        scratch_shapes=[pltpu.VMEM((count, rows, cols), BF16)],
        cost_estimate=pl.CostEstimate(flops=0, bytes_accessed=count * rows * cols * 4, transcendentals=0),
        name="in_order",
    )(spot, *blocks)


def ring_z(start, waits):
    ahead = behind = start
    blocks = [start]
    for step in range(1, 5):
        ahead = shift(ahead, Z, 8, 1)
        if step < 4:
            behind = shift(behind, Z, 8, -1)
            ahead, behind = after([ahead, behind], *waits.get(step, ()))
            blocks += [ahead, behind]
    return blocks + [ahead]


def chunk_squares(read, count, width):
    def step(index, total):
        wide = read(index).astype(F32)
        return total + jnp.sum((wide * wide).reshape(-1, 8, width), axis=0)

    return jnp.sum(lax.fori_loop(0, count, step, jnp.zeros((8, width), F32)), axis=0, keepdims=True)


def attention_kernel(start_ref, q_ref, before_ref, own_ref, o_ref):
    heads = q_ref.shape[0] // HD

    def window(kind, head, block):
        rows = pl.ds(pl.multiple_of((kind * heads + head) * HD, HD), HD)
        ref, block = (before_ref, block) if block < 2 else (own_ref, block - 2)
        return ref[rows, block * BLOCK : (block + 1) * BLOCK]

    key_row = lax.broadcasted_iota(jnp.int32, (BLOCK, BLOCK), 0)
    query_col = lax.broadcasted_iota(jnp.int32, (BLOCK, BLOCK), 1)
    causal = key_row <= query_col

    def one_head(head, carry):
        rows = pl.ds(pl.multiple_of(head * HD, HD), HD)
        for part in range(q_ref.shape[1] // BLOCK):
            cols = slice(part * BLOCK, (part + 1) * BLOCK)
            query = q_ref[rows, cols]
            start = start_ref[:, cols]
            scores = []
            for step in range(3):
                base = (part + step) * BLOCK
                keys = window(0, head, part + step)
                score = lax.dot_general(
                    keys, query, (((0,), (0,)), ((), ())), preferred_element_type=F32
                )
                allowed = key_row >= start - base
                if step == 2:
                    allowed = allowed & causal
                scores.append(jnp.where(allowed, score, -1e30))
            top = jnp.maximum(jnp.maximum(scores[0], scores[1]), scores[2])
            top = jnp.max(top, axis=0, keepdims=True)
            total = jnp.zeros((1, BLOCK), F32)
            mixed = jnp.zeros((HD, BLOCK), F32)
            for step in range(3):
                weight = jnp.exp2((scores[step] - top) * (math.sqrt(HD) * LOG2E))
                total = total + jnp.sum(weight, axis=0, keepdims=True)
                mixed = mixed + jnp.dot(
                    window(1, head, part + step),
                    weight.astype(BF16),
                    preferred_element_type=F32,
                )
            o_ref[rows, cols] = (mixed / total).astype(BF16)
        return carry

    lax.fori_loop(0, heads, one_head, 0)


def attention(start, query, before, own):
    return pl.pallas_call(
        attention_kernel,
        out_shape=jax.ShapeDtypeStruct(query.shape, BF16),
        in_specs=[pl.BlockSpec(memory_space=pltpu.VMEM)] * 4,
        out_specs=pl.BlockSpec(memory_space=pltpu.VMEM),
        cost_estimate=pl.CostEstimate(flops=800_000_000, bytes_accessed=4_000_000, transcendentals=3_000_000),
        name="attention",
    )(start, query, before, own)


def stream_starts(segment):
    order = jnp.arange(segment.shape[0], dtype=jnp.int32)
    earlier = jnp.concatenate([segment[:1], segment[:-1]])
    return lax.cummax(jnp.where(segment != earlier, order, jnp.zeros_like(order)))


def project_kernel(place_ref, *refs):
    x_refs, w_refs, gain_ref, cos_ref, sin_ref = refs[:4], refs[4:12], *refs[12:15]
    query_ref, own_ref, features_ref, size_ref, weight, result = refs[15:]
    tp, ring = place_ref[0], place_ref[2]
    local, rows = query_ref.shape
    for away, ref in enumerate(x_refs):
        block = (tp + away) % 4
        features_ref[pl.ds(pl.multiple_of(block * local, local), local), :] = ref[...]
    for away, ref in zip(RING_ORDER, w_refs):
        weight[(ring + away) % 8] = ref[...]
    size = lax.rsqrt(
        chunk_squares(lambda i: features_ref[pl.ds(pl.multiple_of(i * 128, 128), 128), :], D // 128, rows) + EPS
    )
    size_ref[...] = size
    for kind in range(3):
        part = weight[..., kind * local : (kind + 1) * local].reshape(D, local)
        turned = jnp.transpose(part)
        wide = turned.astype(F32)
        length = lax.rsqrt(jnp.sum(wide * wide, axis=1, keepdims=True) + EPS)
        raw = jnp.dot(turned, features_ref[...], preferred_element_type=F32)
        result[kind * local : (kind + 1) * local] = raw * length * size
    half = HD // 2
    cosine, sine = cos_ref[...], sin_ref[...]

    def one_head(index, carry):
        span = pl.ds(pl.multiple_of(index * HD, HD), HD)
        gain = gain_ref[span, :]
        for kind, target in ((0, query_ref), (1, own_ref)):
            part = result[pl.ds(pl.multiple_of(kind * local + index * HD, HD), HD), :]
            length = lax.rsqrt(jnp.sum(part * part, axis=0, keepdims=True) + EPS)
            part = (gain * (part * length)).astype(BF16).astype(F32)
            first, second = part[:half], part[half:]
            both = [first * cosine - second * sine, first * sine + second * cosine]
            target[span, :] = jnp.concatenate(both, axis=0).astype(BF16)
        spot = pl.ds(pl.multiple_of(local + index * HD, HD), HD)
        own_ref[spot, :] = result[pl.ds(pl.multiple_of(2 * local + index * HD, HD), HD), :].astype(BF16)
        return carry

    lax.fori_loop(0, local // HD, one_head, 0)


def project(spot, blocks, weights, gain, cosine, sine):
    local, rows = blocks[0].shape
    return pl.pallas_call(
        project_kernel,
        out_shape=[
            jax.ShapeDtypeStruct((local, rows), BF16),
            jax.ShapeDtypeStruct((2 * local, rows), BF16),
            jax.ShapeDtypeStruct((D, rows), BF16),
            jax.ShapeDtypeStruct((1, rows), F32),
        ],
        in_specs=[SMALL] + [NEAR] * 15,
        out_specs=[NEAR] * 4,
        scratch_shapes=[
            pltpu.VMEM((8, 160, 3 * local), BF16),
            pltpu.VMEM((3 * local, rows), F32),
        ],
        compiler_params=pltpu.CompilerParams(vmem_limit_bytes=40 * 2**20),
        cost_estimate=pl.CostEstimate(flops=1_900_000_000, bytes_accessed=12_000_000, transcendentals=0),
        name="project",
    )(spot, *blocks, *weights, gain, cosine, sine)


def layer_kernel(place_ref, *refs):
    a_refs, features_ref, size_ref, attn_ref, up_ref, gate_ref = refs[:4], *refs[4:9]
    near_refs, far_refs = refs[9:17], refs[17:25]
    part_ref, mixed_ref, attended, state, turned, inner, weight, sems = refs[25:]
    tp, core, ring = place_ref[0], place_ref[1], place_ref[2]
    local, rows = a_refs[0].shape
    hidden = up_ref.shape[1]
    bounds = (0, D, D + 2 * hidden, D + 3 * hidden)
    copies = []
    for kind in range(3):
        cols = slice(bounds[kind], bounds[kind + 1])
        for side, blocks in ((core, near_refs), (1 - core, far_refs)):
            for away, block in zip(RING_ORDER, blocks):
                target = weight.at[(ring + away) % 8, side, :, cols]
                copies.append(pltpu.make_async_copy(block.at[:, cols], target, sems.at[len(copies)]))
                copies[-1].start()
    for away, ref in enumerate(a_refs):
        attended[away * local : (away + 1) * local] = ref[...]
    for copy in copies[:16]:
        copy.wait()

    def group(index, cols):
        return weight[pl.ds(2 * index, 2), :, :, cols].reshape(local, -1)

    def eighth(index):
        return weight[index, :, :, :D].reshape(D // 8, D)

    out_length = lax.rsqrt(chunk_squares(eighth, 8, D) + EPS)

    def project_out(index, total):
        left = (group(index, slice(0, D)).astype(F32) * out_length).astype(BF16)
        block = jnp.dot(left, attended[...], preferred_element_type=F32)
        state[pl.ds(pl.multiple_of(index * local, local), local), :] = block
        return total + jnp.sum((block * block).reshape(-1, 8, rows), axis=0)

    zero = jnp.zeros((8, rows), F32)
    total = jnp.sum(lax.fori_loop(0, 4, project_out, zero), axis=0, keepdims=True)
    pull = lax.rsqrt(total + EPS)
    size = size_ref[...]

    def mix(index, total):
        span = pl.ds(pl.multiple_of(index * 128, 128), 128)
        before = features_ref[span, :].astype(F32) * size
        mixed = before + attn_ref[span, :] * (state[span, :] * pull - before)
        state[span, :] = mixed
        return total + jnp.sum((mixed * mixed).reshape(-1, 8, rows), axis=0)

    total = jnp.sum(lax.fori_loop(0, D // 128, mix, zero), axis=0, keepdims=True)
    scale = lax.rsqrt(total + EPS)

    def turn(index, carry):
        span = pl.ds(pl.multiple_of(index * 128, 128), 128)
        mixed = state[span, :] * scale
        state[span, :] = mixed
        turned[:, span] = jnp.transpose(mixed).astype(BF16)
        return carry

    lax.fori_loop(0, D // 128, turn, 0)
    mixed_ref[...] = state[pl.ds(pl.multiple_of(tp * local, local), local), :]
    for copy in copies[16:]:
        copy.wait()

    def columns(start, index):
        cols = pl.ds(pl.multiple_of(start + index * BLOCK, BLOCK), BLOCK)
        return weight[..., cols].reshape(D, BLOCK)

    def length(part):
        wide = part.astype(F32)
        return lax.rsqrt(jnp.sum(wide * wide, axis=0, keepdims=True) + EPS)

    def expand(index, carry):
        cols = pl.ds(pl.multiple_of(index * BLOCK, BLOCK), BLOCK)
        up_part, gate_part = columns(D, index), columns(D + hidden, index)
        up = jnp.dot(turned[...], up_part, preferred_element_type=F32)
        gate = jnp.dot(turned[...], gate_part, preferred_element_type=F32)
        up = up * (up_ref[:, cols] * length(up_part) * length(columns(D + 2 * hidden, index)))
        gate = gate * (gate_ref[:, cols] * length(gate_part) * math.sqrt(D))
        inner[:, cols] = (up * (gate / (1.0 + jnp.exp(-gate)))).astype(BF16)
        return carry

    lax.fori_loop(0, hidden // BLOCK, expand, 0)

    def contract(index, carry):
        block = lax.dot_general(
            group(index, slice(D + 2 * hidden, D + 3 * hidden)),
            inner[...],
            (((1,), (1,)), ((), ())),
            preferred_element_type=F32,
        )
        part_ref[index] = block.astype(BF16)
        return carry

    lax.fori_loop(0, 4, contract, 0)


def layer(spot, attended, features, size, attn_step, up_scale, gate_scale, near, far):
    local, rows = attended[0].shape
    hidden = up_scale.shape[1]
    return pl.pallas_call(
        layer_kernel,
        out_shape=[
            jax.ShapeDtypeStruct((4, local, rows), BF16),
            jax.ShapeDtypeStruct((local, rows), F32),
        ],
        in_specs=[SMALL] + [NEAR] * 9 + [FAR] * 16,
        out_specs=[NEAR] * 2,
        scratch_shapes=[
            pltpu.VMEM((D, rows), BF16),
            pltpu.VMEM((D, rows), F32),
            pltpu.VMEM((rows, D), BF16),
            pltpu.VMEM((rows, hidden), BF16),
            pltpu.VMEM((8, 2, 80, D + 3 * hidden), BF16),
            pltpu.SemaphoreType.DMA((48,)),
        ],
        compiler_params=pltpu.CompilerParams(vmem_limit_bytes=56 * 2**20),
        cost_estimate=pl.CostEstimate(flops=10_000_000_000, bytes_accessed=20_000_000, transcendentals=1_000_000),
        name="layer",
    )(spot, *attended, features, size, attn_step, up_scale, gate_scale, *near, *far)


def kernel_order(array):
    shape = array.shape
    parts = array.reshape((shape[0] // 320, 4, 2, 2, SHARD) + shape[1:])
    return jnp.moveaxis(parts, 1, 3).reshape(shape)


def outer_order(array):
    shape = array.shape
    parts = array.reshape((shape[0] // 320, 2, 2, 4, SHARD) + shape[1:])
    return jnp.moveaxis(parts, 3, 1).reshape(shape)


def body(
    tokens,
    qkv_weight,
    out_weight,
    gate_up_weight,
    down_weight,
    qk_scale,
    attn_rate,
    mlp_rate,
    up_scale,
    gate_scale,
    segment_ids,
):
    rows = tokens.shape[1]
    local = tokens.shape[2]
    hidden = gate_up_weight.shape[2]
    tp = lax.axis_index("tp")
    core = lax.axis_index("co")
    spot_y = lax.axis_index("y")
    piece = lax.axis_index("zl") * 2 + core
    spot_z = lax.axis_index("zh") * 2 + lax.axis_index("zl")
    spot = jnp.stack([tp, core, spot_z, spot_y]).astype(jnp.int32)

    qkv = qkv_weight.astype(BF16).reshape(SHARD, 3 * local)
    qkv_y = in_order(spot, 3, four_blocks(qkv, "y"), (0, 1, 2, 3))
    blocks = four_blocks(kernel_order(tokens[0].T), "tp")
    qkv_far = swap_core(qkv_y)
    first = core == 0
    qkv_both = jnp.concatenate(
        [jnp.where(first, qkv_y, qkv_far), jnp.where(first, qkv_far, qkv_y)], axis=0
    )

    starts = stream_starts(segment_ids[0])
    own_first = piece * rows
    own_start = lax.dynamic_slice_in_dim(starts, own_first, rows)
    position = own_first + jnp.arange(rows, dtype=jnp.int32) - own_start
    frequency = jnp.exp(-math.log(10000.0) * jnp.arange(HD // 2, dtype=F32) * 2.0 / HD)
    angles = frequency[:, None] * position.astype(F32)[None]
    window = 2 * BLOCK
    cosine, sine = jnp.cos(angles), jnp.sin(angles)
    key_start = (own_start - own_first + window)[None]
    gain = qk_scale[:, None]
    attn_step = kernel_order(attn_rate)[:, None]
    step_block = lax.dynamic_slice_in_dim(kernel_order(mlp_rate), tp * local, local)[:, None]

    out_rows = four_blocks(out_weight.T.astype(BF16), "tp")
    wide = gate_up_weight.astype(BF16).reshape(SHARD, 2 * hidden)
    rest = jnp.concatenate(out_rows + [wide, down_weight.T.astype(BF16)], axis=1)
    (rest,) = after([rest], qkv_y)
    rest_y = in_order(spot, 3, four_blocks(rest, "y"), (0, 1, 2, 3))

    waits = {1: (blocks[1], blocks[3], cosine, sine, key_start, gain), 2: (blocks[2], attn_step, step_block)}
    qkv_blocks = ring_z(qkv_both, waits)
    (rest_y,) = after([rest_y], *qkv_blocks)
    query, own, features, size = project(spot, blocks, qkv_blocks, gain, cosine, sine)
    before = lax.ppermute(own[:, rows - window :], ("zl", "co"), [(i, i + 1) for i in range(3)])
    attended = attention(key_start, query, before, own)
    everyone = four_blocks(attended, "tp")
    near = ring_z(rest_y, {1: (query,), 2: (attended,), 3: (everyone[1], everyone[3])})
    far = [swap_core(block) for block in near]
    parts, mixed = layer(
        spot, everyone, features, size, attn_step, up_scale[None], gate_scale[None], near, far
    )
    landed = lax.all_to_all(parts, "tp", 0, 0, tiled=True).astype(F32)
    mlp_block = landed[0] + landed[1] + landed[2] + landed[3]

    kept = mixed - step_block * mixed
    moved = step_block * mlp_block
    sums = jnp.stack(
        [
            jnp.sum(mlp_block * mlp_block, axis=0),
            jnp.sum(kept * kept, axis=0),
            jnp.sum(kept * moved, axis=0),
            jnp.sum(moved * moved, axis=0),
        ]
    )
    sums = sum(four_blocks(sums, "tp"))
    pull = lax.rsqrt(sums[0] + EPS)
    length = jnp.maximum(sums[1] + 2.0 * pull * sums[2] + pull * pull * sums[3], 0.0)
    final = math.sqrt(D) * lax.rsqrt(length + EPS)
    result = ((kept + pull[None] * moved) * final[None]).astype(BF16)
    return outer_order(result).T[None]


def solution(mesh):
    fine = Mesh(mesh.devices.reshape(4, 4, 4, 2, 2), ("zh", "y", "tp", "zl", "co"))
    rep, cp = ("zh", "y"), ("zl", "co")
    in_specs = (
        P(rep, cp, "tp"),
        P(rep + cp, None, "tp"),
        P("tp", rep + cp),
        P(rep + cp, None, "tp"),
        P("tp", rep + cp),
        P("tp"),
        P(),
        P(),
        P("tp"),
        P("tp"),
        P(rep, None),
    )
    return jax.shard_map(
        body, mesh=fine, in_specs=in_specs, out_specs=P(rep, cp, "tp"), check_vma=False
    )
```

```python
import functools
import math

import jax
import jax.numpy as jnp
from jax import lax
from jax.experimental import pallas as pl
from jax.experimental.pallas import tpu as pltpu
from jax.sharding import Mesh, PartitionSpec as P

D = 1280
HD = 64
EPS = 1e-06
F32 = jnp.float32
BF16 = jnp.bfloat16
Z = ("zh", "zl")
BLOCK = 256
LOG2E = 1.4426950408889634


def ring(count, step):
    return [(i, (i + step) % count) for i in range(count)]


def shift(block, axis, count, step):
    return lax.ppermute(block, axis, ring(count, step))


def swap_core(block):
    return lax.ppermute(block, "co", [(0, 1), (1, 0)])


SHARD = 20
PADDED = 24
WIDE = 64 * PADDED
RING_ORDER = (0, 7, 1, 6, 2, 5, 3, 4)
SMALL = pl.BlockSpec(memory_space=pltpu.SMEM)
NEAR = pl.BlockSpec(memory_space=pltpu.VMEM)
FAR = pl.BlockSpec(memory_space=pl.ANY)


def four_blocks(block, axis):
    return [block] + [shift(block, axis, 4, 4 - away) for away in (1, 2, 3)]


def after(blocks, *earlier):
    return list(lax.optimization_barrier((tuple(blocks), earlier))[0])


def order_kernel(which, aways, place_ref, *refs):
    count = len(aways)
    blocks, whole_ref, held = refs[:count], refs[count], refs[count + 1]
    me = place_ref[which]
    for block, away in zip(blocks, aways):
        held[(me + away) % count] = block[...]
    whole_ref[...] = jnp.concatenate([held[slot] for slot in range(count)], axis=0)


def in_order(spot, which, blocks, aways):
    rows, cols = blocks[0].shape
    count = len(blocks)
    return pl.pallas_call(
        functools.partial(order_kernel, which, aways),
        out_shape=jax.ShapeDtypeStruct((count * rows, cols), BF16),
        in_specs=[SMALL] + [NEAR] * count,
        out_specs=NEAR,
        scratch_shapes=[pltpu.VMEM((count, rows, cols), BF16)],
        cost_estimate=pl.CostEstimate(flops=0, bytes_accessed=count * rows * cols * 4, transcendentals=0),
        name="in_order",
    )(spot, *blocks)


def ring_z(start, ahead, behind, waits):
    blocks = [start]
    for step in range(1, 4):
        ahead, behind = after([ahead, behind], *waits.get(step, ()))
        blocks += [ahead, behind]
        ahead = shift(ahead, Z, 8, 1)
        if step < 3:
            behind = shift(behind, Z, 8, -1)
    return blocks + [ahead]


def chunk_squares(read, count, width):
    def step(index, total):
        wide = read(index).astype(F32)
        return total + jnp.sum((wide * wide).reshape(-1, 8, width), axis=0)

    return jnp.sum(lax.fori_loop(0, count, step, jnp.zeros((8, width), F32)), axis=0, keepdims=True)


def attention_kernel(start_ref, q_ref, before_ref, own_ref, o_ref):
    heads = q_ref.shape[0] // HD

    def window(kind, head, block):
        rows = pl.ds(pl.multiple_of((kind * heads + head) * HD, HD), HD)
        ref, block = (before_ref, block) if block < 2 else (own_ref, block - 2)
        return ref[rows, block * BLOCK : (block + 1) * BLOCK]

    key_row = lax.broadcasted_iota(jnp.int32, (BLOCK, BLOCK), 0)
    query_col = lax.broadcasted_iota(jnp.int32, (BLOCK, BLOCK), 1)
    causal = key_row <= query_col

    def one_head(head, carry):
        rows = pl.ds(pl.multiple_of(head * HD, HD), HD)
        for part in range(q_ref.shape[1] // BLOCK):
            cols = slice(part * BLOCK, (part + 1) * BLOCK)
            query = q_ref[rows, cols]
            start = start_ref[:, cols]
            scores = []
            for step in range(3):
                base = (part + step) * BLOCK
                keys = window(0, head, part + step)
                score = lax.dot_general(
                    keys, query, (((0,), (0,)), ((), ())), preferred_element_type=F32
                )
                allowed = key_row >= start - base
                if step == 2:
                    allowed = allowed & causal
                scores.append(jnp.where(allowed, score, -1e30))
            top = jnp.maximum(jnp.maximum(scores[0], scores[1]), scores[2])
            top = jnp.max(top, axis=0, keepdims=True)
            total = jnp.zeros((1, BLOCK), F32)
            mixed = jnp.zeros((HD, BLOCK), F32)
            for step in range(3):
                weight = jnp.exp2((scores[step] - top) * (math.sqrt(HD) * LOG2E))
                total = total + jnp.sum(weight, axis=0, keepdims=True)
                mixed = mixed + jnp.dot(
                    window(1, head, part + step),
                    weight.astype(BF16),
                    preferred_element_type=F32,
                )
            o_ref[rows, cols] = (mixed / total).astype(BF16)
        return carry

    lax.fori_loop(0, heads, one_head, 0)


def attention(start, query, before, own):
    return pl.pallas_call(
        attention_kernel,
        out_shape=jax.ShapeDtypeStruct(query.shape, BF16),
        in_specs=[pl.BlockSpec(memory_space=pltpu.VMEM)] * 4,
        out_specs=pl.BlockSpec(memory_space=pltpu.VMEM),
        cost_estimate=pl.CostEstimate(flops=800_000_000, bytes_accessed=4_000_000, transcendentals=3_000_000),
        name="attention",
    )(start, query, before, own)


def stream_starts(segment):
    order = jnp.arange(segment.shape[0], dtype=jnp.int32)
    earlier = jnp.concatenate([segment[:1], segment[:-1]])
    return lax.cummax(jnp.where(segment != earlier, order, jnp.zeros_like(order)))


def project_kernel(place_ref, *refs):
    x_refs, near_refs, far_refs, gain_ref, cos_ref, sin_ref = refs[:4], refs[4:8], refs[8], *refs[9:12]
    query_ref, own_ref, features_ref, size_ref, held, weight, result = refs[12:]
    tp, core, spot_y = place_ref[0], place_ref[1], place_ref[3]
    local, rows = query_ref.shape
    held[...] = jnp.zeros_like(held)
    for away, ref in enumerate(x_refs):
        block = (tp + away) % 4
        features_ref[pl.ds(pl.multiple_of(block * local, local), local), :] = ref[...]
        for shard in range(16):
            held[block, shard, :SHARD] = ref[shard * SHARD : (shard + 1) * SHARD]
    for away, ref in enumerate(near_refs):
        y = (spot_y + away) % 4
        for z in range(8):
            weight[z, core, y] = ref[z]
            weight[z, 1 - core, y] = far_refs[away, z]
    size = lax.rsqrt(
        chunk_squares(lambda i: features_ref[pl.ds(pl.multiple_of(i * 128, 128), 128), :], D // 128, rows) + EPS
    )
    size_ref[...] = size
    for kind in range(3):
        part = weight[..., kind * local : (kind + 1) * local].reshape(WIDE, local)
        turned = jnp.transpose(part)
        wide = turned.astype(F32)
        length = lax.rsqrt(jnp.sum(wide * wide, axis=1, keepdims=True) + EPS)
        raw = jnp.dot(turned, held[...].reshape(WIDE, rows), preferred_element_type=F32)
        result[kind * local : (kind + 1) * local] = raw * length * size
    half = HD // 2
    cosine, sine = cos_ref[...], sin_ref[...]

    def one_head(index, carry):
        span = pl.ds(pl.multiple_of(index * HD, HD), HD)
        gain = gain_ref[span, :]
        for kind, target in ((0, query_ref), (1, own_ref)):
            part = result[pl.ds(pl.multiple_of(kind * local + index * HD, HD), HD), :]
            length = lax.rsqrt(jnp.sum(part * part, axis=0, keepdims=True) + EPS)
            part = (gain * (part * length)).astype(BF16).astype(F32)
            first, second = part[:half], part[half:]
            both = [first * cosine - second * sine, first * sine + second * cosine]
            target[span, :] = jnp.concatenate(both, axis=0).astype(BF16)
        spot = pl.ds(pl.multiple_of(local + index * HD, HD), HD)
        own_ref[spot, :] = result[pl.ds(pl.multiple_of(2 * local + index * HD, HD), HD), :].astype(BF16)
        return carry

    lax.fori_loop(0, local // HD, one_head, 0)


def project(spot, blocks, near, far, gain, cosine, sine):
    local, rows = blocks[0].shape
    return pl.pallas_call(
        project_kernel,
        out_shape=[
            jax.ShapeDtypeStruct((local, rows), BF16),
            jax.ShapeDtypeStruct((2 * local, rows), BF16),
            jax.ShapeDtypeStruct((D, rows), BF16),
            jax.ShapeDtypeStruct((1, rows), F32),
        ],
        in_specs=[SMALL] + [NEAR] * 12,
        out_specs=[NEAR] * 4,
        scratch_shapes=[
            pltpu.VMEM((4, 16, PADDED, rows), BF16),
            pltpu.VMEM((8, 2, 4, PADDED, 3 * local), BF16),
            pltpu.VMEM((3 * local, rows), F32),
        ],
        compiler_params=pltpu.CompilerParams(vmem_limit_bytes=40 * 2**20),
        cost_estimate=pl.CostEstimate(flops=1_900_000_000, bytes_accessed=12_000_000, transcendentals=0),
        name="project",
    )(spot, *blocks, *near, far, gain, cosine, sine)


def layer_kernel(place_ref, *refs):
    a_refs, features_ref, size_ref, attn_ref, up_ref, gate_ref = refs[:4], *refs[4:9]
    near_refs, far_refs = refs[9:17], refs[17:25]
    part_ref, mixed_ref, attended, state, turned, inner, weight, sems = refs[25:]
    tp, core, ring = place_ref[0], place_ref[1], place_ref[2]
    local, rows = a_refs[0].shape
    hidden = up_ref.shape[1]
    bounds = (0, D, D + 2 * hidden, D + 3 * hidden)
    copies = []
    for kind in range(3):
        cols = slice(bounds[kind], bounds[kind + 1])
        for side, blocks in ((core, near_refs), (1 - core, far_refs)):
            for away, block in zip(RING_ORDER, blocks):
                target = weight.at[(ring + away) % 8, side, :, cols]
                copies.append(pltpu.make_async_copy(block.at[:, cols], target, sems.at[len(copies)]))
                copies[-1].start()
    for away, ref in enumerate(a_refs):
        attended[away * local : (away + 1) * local] = ref[...]
    for copy in copies[:16]:
        copy.wait()

    def group(index, cols):
        return weight[pl.ds(2 * index, 2), :, :, cols].reshape(local, -1)

    def eighth(index):
        return weight[index, :, :, :D].reshape(D // 8, D)

    out_length = lax.rsqrt(chunk_squares(eighth, 8, D) + EPS)

    def project_out(index, total):
        left = (group(index, slice(0, D)).astype(F32) * out_length).astype(BF16)
        block = jnp.dot(left, attended[...], preferred_element_type=F32)
        state[pl.ds(pl.multiple_of(index * local, local), local), :] = block
        return total + jnp.sum((block * block).reshape(-1, 8, rows), axis=0)

    zero = jnp.zeros((8, rows), F32)
    total = jnp.sum(lax.fori_loop(0, 4, project_out, zero), axis=0, keepdims=True)
    pull = lax.rsqrt(total + EPS)
    size = size_ref[...]

    def mix(index, total):
        span = pl.ds(pl.multiple_of(index * 128, 128), 128)
        before = features_ref[span, :].astype(F32) * size
        mixed = before + attn_ref[span, :] * (state[span, :] * pull - before)
        state[span, :] = mixed
        return total + jnp.sum((mixed * mixed).reshape(-1, 8, rows), axis=0)

    total = jnp.sum(lax.fori_loop(0, D // 128, mix, zero), axis=0, keepdims=True)
    scale = lax.rsqrt(total + EPS)

    def turn(index, carry):
        span = pl.ds(pl.multiple_of(index * 128, 128), 128)
        mixed = state[span, :] * scale
        state[span, :] = mixed
        turned[:, span] = jnp.transpose(mixed).astype(BF16)
        return carry

    lax.fori_loop(0, D // 128, turn, 0)
    mixed_ref[...] = state[pl.ds(pl.multiple_of(tp * local, local), local), :]
    for copy in copies[16:]:
        copy.wait()

    def columns(start, index):
        cols = pl.ds(pl.multiple_of(start + index * BLOCK, BLOCK), BLOCK)
        return weight[..., cols].reshape(D, BLOCK)

    def length(part):
        wide = part.astype(F32)
        return lax.rsqrt(jnp.sum(wide * wide, axis=0, keepdims=True) + EPS)

    def expand(index, carry):
        cols = pl.ds(pl.multiple_of(index * BLOCK, BLOCK), BLOCK)
        up_part, gate_part = columns(D, index), columns(D + hidden, index)
        up = jnp.dot(turned[...], up_part, preferred_element_type=F32)
        gate = jnp.dot(turned[...], gate_part, preferred_element_type=F32)
        up = up * (up_ref[:, cols] * length(up_part) * length(columns(D + 2 * hidden, index)))
        gate = gate * (gate_ref[:, cols] * length(gate_part) * math.sqrt(D))
        inner[:, cols] = (up * (gate / (1.0 + jnp.exp(-gate)))).astype(BF16)
        return carry

    lax.fori_loop(0, hidden // BLOCK, expand, 0)

    def contract(index, carry):
        block = lax.dot_general(
            group(index, slice(D + 2 * hidden, D + 3 * hidden)),
            inner[...],
            (((1,), (1,)), ((), ())),
            preferred_element_type=F32,
        )
        part_ref[index] = block.astype(BF16)
        return carry

    lax.fori_loop(0, 4, contract, 0)


def layer(spot, attended, features, size, attn_step, up_scale, gate_scale, near, far):
    local, rows = attended[0].shape
    hidden = up_scale.shape[1]
    return pl.pallas_call(
        layer_kernel,
        out_shape=[
            jax.ShapeDtypeStruct((4, local, rows), BF16),
            jax.ShapeDtypeStruct((local, rows), F32),
        ],
        in_specs=[SMALL] + [NEAR] * 9 + [FAR] * 16,
        out_specs=[NEAR] * 2,
        scratch_shapes=[
            pltpu.VMEM((D, rows), BF16),
            pltpu.VMEM((D, rows), F32),
            pltpu.VMEM((rows, D), BF16),
            pltpu.VMEM((rows, hidden), BF16),
            pltpu.VMEM((8, 2, 80, D + 3 * hidden), BF16),
            pltpu.SemaphoreType.DMA((48,)),
        ],
        compiler_params=pltpu.CompilerParams(vmem_limit_bytes=56 * 2**20),
        cost_estimate=pl.CostEstimate(flops=10_000_000_000, bytes_accessed=20_000_000, transcendentals=1_000_000),
        name="layer",
    )(spot, *attended, features, size, attn_step, up_scale, gate_scale, *near, *far)


def kernel_order(array):
    shape = array.shape
    parts = array.reshape((shape[0] // 320, 4, 2, 2, SHARD) + shape[1:])
    return jnp.moveaxis(parts, 1, 3).reshape(shape)


def outer_order(array):
    shape = array.shape
    parts = array.reshape((shape[0] // 320, 2, 2, 4, SHARD) + shape[1:])
    return jnp.moveaxis(parts, 3, 1).reshape(shape)


def body(
    tokens,
    qkv_weight,
    out_weight,
    gate_up_weight,
    down_weight,
    qk_scale,
    attn_rate,
    mlp_rate,
    up_scale,
    gate_scale,
    segment_ids,
):
    rows = tokens.shape[1]
    local = tokens.shape[2]
    hidden = gate_up_weight.shape[2]
    tp = lax.axis_index("tp")
    core = lax.axis_index("co")
    spot_y = lax.axis_index("y")
    piece = lax.axis_index("zl") * 2 + core
    spot_z = lax.axis_index("zh") * 2 + lax.axis_index("zl")
    spot = jnp.stack([tp, core, spot_z, spot_y]).astype(jnp.int32)

    qkv = jnp.pad(qkv_weight.astype(BF16).reshape(SHARD, 3 * local), ((0, PADDED - SHARD), (0, 0)))
    everywhere = jnp.broadcast_to(qkv[None], (8,) + qkv.shape)
    qkv_z = lax.all_to_all(everywhere, Z, 0, 0, tiled=True)
    blocks = four_blocks(kernel_order(tokens[0].T), "tp")

    starts = stream_starts(segment_ids[0])
    own_first = piece * rows
    own_start = lax.dynamic_slice_in_dim(starts, own_first, rows)
    position = own_first + jnp.arange(rows, dtype=jnp.int32) - own_start
    frequency = jnp.exp(-math.log(10000.0) * jnp.arange(HD // 2, dtype=F32) * 2.0 / HD)
    angles = frequency[:, None] * position.astype(F32)[None]
    window = 2 * BLOCK
    cosine, sine = jnp.cos(angles), jnp.sin(angles)
    key_start = (own_start - own_first + window)[None]
    gain = qk_scale[:, None]
    attn_step = kernel_order(attn_rate)[:, None]
    step_block = lax.dynamic_slice_in_dim(kernel_order(mlp_rate), tp * local, local)[:, None]

    out_rows = four_blocks(out_weight.T.astype(BF16), "tp")
    wide = gate_up_weight.astype(BF16).reshape(SHARD, 2 * hidden)
    rest = jnp.concatenate(out_rows + [wide, down_weight.T.astype(BF16)], axis=1)
    rest_y = in_order(spot, 3, four_blocks(rest, "y"), (0, 1, 2, 3))

    (qkv_z,) = after([qkv_z], rest_y, cosine, sine, key_start, gain, attn_step, step_block, *blocks)
    qkv_near = four_blocks(qkv_z, "y")
    ahead, behind = shift(rest_y, Z, 8, 1), shift(rest_y, Z, 8, -1)
    (qkv_stack,) = after([jnp.stack(qkv_near)], ahead, behind)
    qkv_far = swap_core(qkv_stack)
    query, own, features, size = project(spot, blocks, qkv_near, qkv_far, gain, cosine, sine)
    before = lax.ppermute(own[:, rows - window :], ("zl", "co"), [(i, i + 1) for i in range(3)])
    attended = attention(key_start, query, before, own)
    everyone = four_blocks(attended, "tp")
    near = ring_z(rest_y, ahead, behind, {1: (qkv_far,), 2: (attended,), 3: (everyone[1], everyone[3])})
    far = [swap_core(block) for block in near]
    parts, mixed = layer(
        spot, everyone, features, size, attn_step, up_scale[None], gate_scale[None], near, far
    )
    landed = lax.all_to_all(parts, "tp", 0, 0, tiled=True).astype(F32)
    mlp_block = landed[0] + landed[1] + landed[2] + landed[3]

    kept = mixed - step_block * mixed
    moved = step_block * mlp_block
    sums = jnp.stack(
        [
            jnp.sum(mlp_block * mlp_block, axis=0),
            jnp.sum(kept * kept, axis=0),
            jnp.sum(kept * moved, axis=0),
            jnp.sum(moved * moved, axis=0),
        ]
    )
    sums = sum(four_blocks(sums, "tp"))
    pull = lax.rsqrt(sums[0] + EPS)
    length = jnp.maximum(sums[1] + 2.0 * pull * sums[2] + pull * pull * sums[3], 0.0)
    final = math.sqrt(D) * lax.rsqrt(length + EPS)
    result = ((kept + pull[None] * moved) * final[None]).astype(BF16)
    return outer_order(result).T[None]


def solution(mesh):
    fine = Mesh(mesh.devices.reshape(4, 4, 4, 2, 2), ("zh", "y", "tp", "zl", "co"))
    rep, cp = ("zh", "y"), ("zl", "co")
    in_specs = (
        P(rep, cp, "tp"),
        P(rep + cp, None, "tp"),
        P("tp", rep + cp),
        P(rep + cp, None, "tp"),
        P("tp", rep + cp),
        P("tp"),
        P(),
        P(),
        P("tp"),
        P("tp"),
        P(rep, None),
    )
    return jax.shard_map(
        body, mesh=fine, in_specs=in_specs, out_specs=P(rep, cp, "tp"), check_vma=False
    )
```

```python
import functools
import math

import jax
import jax.numpy as jnp
from jax import lax
from jax.experimental import pallas as pl
from jax.experimental.pallas import tpu as pltpu
from jax.sharding import Mesh, PartitionSpec as P

D = 1280
HD = 64
EPS = 1e-06
F32 = jnp.float32
BF16 = jnp.bfloat16
Z = ("zh", "zl")
BLOCK = 256
LOG2E = 1.4426950408889634


def ring(count, step):
    return [(i, (i + step) % count) for i in range(count)]


def shift(block, axis, count, step):
    return lax.ppermute(block, axis, ring(count, step))


def swap_core(block):
    return lax.ppermute(block, "co", [(0, 1), (1, 0)])


SHARD = 20
PADDED = 24
WIDE = 64 * PADDED
RING_ORDER = (0, 7, 1, 6, 2, 5, 3, 4)
SMALL = pl.BlockSpec(memory_space=pltpu.SMEM)
NEAR = pl.BlockSpec(memory_space=pltpu.VMEM)
FAR = pl.BlockSpec(memory_space=pl.ANY)


def four_blocks(block, axis):
    return [block] + [shift(block, axis, 4, 4 - away) for away in (1, 2, 3)]


def after(blocks, *earlier):
    return list(lax.optimization_barrier((tuple(blocks), earlier))[0])


def order_kernel(which, aways, place_ref, *refs):
    count = len(aways)
    blocks, whole_ref, held = refs[:count], refs[count], refs[count + 1]
    me = place_ref[which]
    for block, away in zip(blocks, aways):
        held[(me + away) % count] = block[...]
    whole_ref[...] = jnp.concatenate([held[slot] for slot in range(count)], axis=0)


def in_order(spot, which, blocks, aways):
    rows, cols = blocks[0].shape
    count = len(blocks)
    return pl.pallas_call(
        functools.partial(order_kernel, which, aways),
        out_shape=jax.ShapeDtypeStruct((count * rows, cols), BF16),
        in_specs=[SMALL] + [NEAR] * count,
        out_specs=NEAR,
        scratch_shapes=[pltpu.VMEM((count, rows, cols), BF16)],
        cost_estimate=pl.CostEstimate(flops=0, bytes_accessed=count * rows * cols * 4, transcendentals=0),
        name="in_order",
    )(spot, *blocks)


def ring_z(start, ahead, behind, waits):
    blocks = [start]
    for step in range(1, 4):
        ahead, behind = after([ahead, behind], *waits.get(step, ()))
        blocks += [ahead, behind]
        ahead = shift(ahead, Z, 8, 1)
        if step < 3:
            behind = shift(behind, Z, 8, -1)
    return blocks + [ahead]


def chunk_squares(read, count, width):
    def step(index, total):
        wide = read(index).astype(F32)
        return total + jnp.sum((wide * wide).reshape(-1, 8, width), axis=0)

    return jnp.sum(lax.fori_loop(0, count, step, jnp.zeros((8, width), F32)), axis=0, keepdims=True)


def attention_kernel(start_ref, q_ref, before_ref, own_ref, o_ref):
    heads = q_ref.shape[0] // HD

    def window(kind, head, block):
        rows = pl.ds(pl.multiple_of((kind * heads + head) * HD, HD), HD)
        ref, block = (before_ref, block) if block < 2 else (own_ref, block - 2)
        return ref[rows, block * BLOCK : (block + 1) * BLOCK]

    key_row = lax.broadcasted_iota(jnp.int32, (BLOCK, BLOCK), 0)
    query_col = lax.broadcasted_iota(jnp.int32, (BLOCK, BLOCK), 1)
    causal = key_row <= query_col

    def one_head(head, carry):
        rows = pl.ds(pl.multiple_of(head * HD, HD), HD)
        for part in range(q_ref.shape[1] // BLOCK):
            cols = slice(part * BLOCK, (part + 1) * BLOCK)
            query = q_ref[rows, cols]
            start = start_ref[:, cols]
            scores = []
            for step in range(3):
                base = (part + step) * BLOCK
                keys = window(0, head, part + step)
                score = lax.dot_general(
                    keys, query, (((0,), (0,)), ((), ())), preferred_element_type=F32
                )
                allowed = key_row >= start - base
                if step == 2:
                    allowed = allowed & causal
                scores.append(jnp.where(allowed, score, -1e30))
            top = jnp.maximum(jnp.maximum(scores[0], scores[1]), scores[2])
            top = jnp.max(top, axis=0, keepdims=True)
            total = jnp.zeros((1, BLOCK), F32)
            mixed = jnp.zeros((HD, BLOCK), F32)
            for step in range(3):
                weight = jnp.exp2((scores[step] - top) * (math.sqrt(HD) * LOG2E))
                total = total + jnp.sum(weight, axis=0, keepdims=True)
                mixed = mixed + jnp.dot(
                    window(1, head, part + step),
                    weight.astype(BF16),
                    preferred_element_type=F32,
                )
            o_ref[rows, cols] = (mixed / total).astype(BF16)
        return carry

    lax.fori_loop(0, heads, one_head, 0)


def attention(start, query, before, own):
    return pl.pallas_call(
        attention_kernel,
        out_shape=jax.ShapeDtypeStruct(query.shape, BF16),
        in_specs=[pl.BlockSpec(memory_space=pltpu.VMEM)] * 4,
        out_specs=pl.BlockSpec(memory_space=pltpu.VMEM),
        cost_estimate=pl.CostEstimate(flops=800_000_000, bytes_accessed=4_000_000, transcendentals=3_000_000),
        name="attention",
    )(start, query, before, own)


def stream_starts(segment):
    order = jnp.arange(segment.shape[0], dtype=jnp.int32)
    earlier = jnp.concatenate([segment[:1], segment[:-1]])
    return lax.cummax(jnp.where(segment != earlier, order, jnp.zeros_like(order)))


def project_kernel(place_ref, *refs):
    x_refs, near_refs, far_refs, gain_ref, cos_ref, sin_ref = refs[:4], refs[4:8], refs[8], *refs[9:12]
    query_ref, own_ref, features_ref, size_ref, held, weight, result = refs[12:]
    tp, core, spot_y = place_ref[0], place_ref[1], place_ref[3]
    local, rows = query_ref.shape
    held[...] = jnp.zeros_like(held)
    for away, ref in enumerate(x_refs):
        block = (tp + away) % 4
        features_ref[pl.ds(pl.multiple_of(block * local, local), local), :] = ref[...]
        for shard in range(16):
            held[block, shard, :SHARD] = ref[shard * SHARD : (shard + 1) * SHARD]
    for away, ref in enumerate(near_refs):
        y = (spot_y + away) % 4
        for z in range(8):
            weight[z, core, y] = ref[z]
            weight[z, 1 - core, y] = far_refs[away, z]
    size = lax.rsqrt(
        chunk_squares(lambda i: features_ref[pl.ds(pl.multiple_of(i * 128, 128), 128), :], D // 128, rows) + EPS
    )
    size_ref[...] = size
    for kind in range(3):
        part = weight[..., kind * local : (kind + 1) * local].reshape(WIDE, local)
        turned = jnp.transpose(part)
        wide = turned.astype(F32)
        length = lax.rsqrt(jnp.sum(wide * wide, axis=1, keepdims=True) + EPS)
        raw = jnp.dot(turned, held[...].reshape(WIDE, rows), preferred_element_type=F32)
        result[kind * local : (kind + 1) * local] = raw * length * size
    half = HD // 2
    cosine, sine = cos_ref[...], sin_ref[...]

    def one_head(index, carry):
        span = pl.ds(pl.multiple_of(index * HD, HD), HD)
        gain = gain_ref[span, :]
        for kind, target in ((0, query_ref), (1, own_ref)):
            part = result[pl.ds(pl.multiple_of(kind * local + index * HD, HD), HD), :]
            length = lax.rsqrt(jnp.sum(part * part, axis=0, keepdims=True) + EPS)
            part = (gain * (part * length)).astype(BF16).astype(F32)
            first, second = part[:half], part[half:]
            both = [first * cosine - second * sine, first * sine + second * cosine]
            target[span, :] = jnp.concatenate(both, axis=0).astype(BF16)
        spot = pl.ds(pl.multiple_of(local + index * HD, HD), HD)
        own_ref[spot, :] = result[pl.ds(pl.multiple_of(2 * local + index * HD, HD), HD), :].astype(BF16)
        return carry

    lax.fori_loop(0, local // HD, one_head, 0)


def project(spot, blocks, near, far, gain, cosine, sine):
    local, rows = blocks[0].shape
    return pl.pallas_call(
        project_kernel,
        out_shape=[
            jax.ShapeDtypeStruct((local, rows), BF16),
            jax.ShapeDtypeStruct((2 * local, rows), BF16),
            jax.ShapeDtypeStruct((D, rows), BF16),
            jax.ShapeDtypeStruct((1, rows), F32),
        ],
        in_specs=[SMALL] + [NEAR] * 12,
        out_specs=[NEAR] * 4,
        scratch_shapes=[
            pltpu.VMEM((4, 16, PADDED, rows), BF16),
            pltpu.VMEM((8, 2, 4, PADDED, 3 * local), BF16),
            pltpu.VMEM((3 * local, rows), F32),
        ],
        compiler_params=pltpu.CompilerParams(vmem_limit_bytes=40 * 2**20),
        cost_estimate=pl.CostEstimate(flops=1_900_000_000, bytes_accessed=12_000_000, transcendentals=0),
        name="project",
    )(spot, *blocks, *near, far, gain, cosine, sine)


def layer_kernel(place_ref, *refs):
    a_refs, features_ref, size_ref, attn_ref, up_ref, gate_ref = refs[:4], *refs[4:9]
    near_refs, far_refs = refs[9:17], refs[17:25]
    part_ref, mixed_ref, attended, state, turned, inner, weight, sems = refs[25:]
    tp, core, ring = place_ref[0], place_ref[1], place_ref[2]
    local, rows = a_refs[0].shape
    hidden = up_ref.shape[1]
    bounds = (0, D, D + 2 * hidden, D + 3 * hidden)
    copies = []
    for kind in range(3):
        cols = slice(bounds[kind], bounds[kind + 1])
        for side, blocks in ((core, near_refs), (1 - core, far_refs)):
            for away, block in zip(RING_ORDER, blocks):
                target = weight.at[(ring + away) % 8, side, :, cols]
                copies.append(pltpu.make_async_copy(block.at[:, cols], target, sems.at[len(copies)]))
                copies[-1].start()
    for away, ref in enumerate(a_refs):
        attended[away * local : (away + 1) * local] = ref[...]
    for copy in copies[:16]:
        copy.wait()

    def group(index, cols):
        return weight[pl.ds(2 * index, 2), :, :, cols].reshape(local, -1)

    def eighth(index):
        return weight[index, :, :, :D].reshape(D // 8, D)

    out_length = lax.rsqrt(chunk_squares(eighth, 8, D) + EPS)

    def project_out(index, total):
        left = (group(index, slice(0, D)).astype(F32) * out_length).astype(BF16)
        block = jnp.dot(left, attended[...], preferred_element_type=F32)
        state[pl.ds(pl.multiple_of(index * local, local), local), :] = block
        return total + jnp.sum((block * block).reshape(-1, 8, rows), axis=0)

    zero = jnp.zeros((8, rows), F32)
    total = jnp.sum(lax.fori_loop(0, 4, project_out, zero), axis=0, keepdims=True)
    pull = lax.rsqrt(total + EPS)
    size = size_ref[...]

    def mix(index, total):
        span = pl.ds(pl.multiple_of(index * 128, 128), 128)
        before = features_ref[span, :].astype(F32) * size
        mixed = before + attn_ref[span, :] * (state[span, :] * pull - before)
        state[span, :] = mixed
        return total + jnp.sum((mixed * mixed).reshape(-1, 8, rows), axis=0)

    total = jnp.sum(lax.fori_loop(0, D // 128, mix, zero), axis=0, keepdims=True)
    scale = lax.rsqrt(total + EPS)

    def turn(index, carry):
        span = pl.ds(pl.multiple_of(index * 128, 128), 128)
        mixed = state[span, :] * scale
        state[span, :] = mixed
        turned[:, span] = jnp.transpose(mixed).astype(BF16)
        return carry

    lax.fori_loop(0, D // 128, turn, 0)
    mixed_ref[...] = state[pl.ds(pl.multiple_of(tp * local, local), local), :]
    for copy in copies[16:]:
        copy.wait()

    def columns(start, index):
        cols = pl.ds(pl.multiple_of(start + index * BLOCK, BLOCK), BLOCK)
        return weight[..., cols].reshape(D, BLOCK)

    def length(part):
        wide = part.astype(F32)
        return lax.rsqrt(jnp.sum(wide * wide, axis=0, keepdims=True) + EPS)

    def expand(index, carry):
        cols = pl.ds(pl.multiple_of(index * BLOCK, BLOCK), BLOCK)
        up_part, gate_part = columns(D, index), columns(D + hidden, index)
        up = jnp.dot(turned[...], up_part, preferred_element_type=F32)
        gate = jnp.dot(turned[...], gate_part, preferred_element_type=F32)
        up = up * (up_ref[:, cols] * length(up_part) * length(columns(D + 2 * hidden, index)))
        gate = gate * (gate_ref[:, cols] * length(gate_part) * math.sqrt(D))
        inner[:, cols] = (up * (gate / (1.0 + jnp.exp(-gate)))).astype(BF16)
        return carry

    lax.fori_loop(0, hidden // BLOCK, expand, 0)

    def contract(index, carry):
        block = lax.dot_general(
            group(index, slice(D + 2 * hidden, D + 3 * hidden)),
            inner[...],
            (((1,), (1,)), ((), ())),
            preferred_element_type=F32,
        )
        part_ref[index] = block.astype(BF16)
        return carry

    lax.fori_loop(0, 4, contract, 0)


def layer(spot, attended, features, size, attn_step, up_scale, gate_scale, near, far):
    local, rows = attended[0].shape
    hidden = up_scale.shape[1]
    return pl.pallas_call(
        layer_kernel,
        out_shape=[
            jax.ShapeDtypeStruct((4, local, rows), BF16),
            jax.ShapeDtypeStruct((local, rows), F32),
        ],
        in_specs=[SMALL] + [NEAR] * 9 + [FAR] * 16,
        out_specs=[NEAR] * 2,
        scratch_shapes=[
            pltpu.VMEM((D, rows), BF16),
            pltpu.VMEM((D, rows), F32),
            pltpu.VMEM((rows, D), BF16),
            pltpu.VMEM((rows, hidden), BF16),
            pltpu.VMEM((8, 2, 80, D + 3 * hidden), BF16),
            pltpu.SemaphoreType.DMA((48,)),
        ],
        compiler_params=pltpu.CompilerParams(vmem_limit_bytes=56 * 2**20),
        cost_estimate=pl.CostEstimate(flops=10_000_000_000, bytes_accessed=20_000_000, transcendentals=1_000_000),
        name="layer",
    )(spot, *attended, features, size, attn_step, up_scale, gate_scale, *near, *far)


def kernel_order(array):
    shape = array.shape
    parts = array.reshape((shape[0] // 320, 4, 2, 2, SHARD) + shape[1:])
    return jnp.moveaxis(parts, 1, 3).reshape(shape)


def outer_order(array):
    shape = array.shape
    parts = array.reshape((shape[0] // 320, 2, 2, 4, SHARD) + shape[1:])
    return jnp.moveaxis(parts, 3, 1).reshape(shape)


def body(
    tokens,
    qkv_weight,
    out_weight,
    gate_up_weight,
    down_weight,
    qk_scale,
    attn_rate,
    mlp_rate,
    up_scale,
    gate_scale,
    segment_ids,
):
    rows = tokens.shape[1]
    local = tokens.shape[2]
    hidden = gate_up_weight.shape[2]
    tp = lax.axis_index("tp")
    core = lax.axis_index("co")
    spot_y = lax.axis_index("y")
    piece = lax.axis_index("zl") * 2 + core
    spot_z = lax.axis_index("zh") * 2 + lax.axis_index("zl")
    spot = jnp.stack([tp, core, spot_z, spot_y]).astype(jnp.int32)

    out_rows = four_blocks(out_weight.T.astype(BF16), "tp")
    shard, own_tokens = after([qkv_weight.astype(BF16), tokens[0].T], *out_rows)
    qkv = jnp.pad(shard.reshape(SHARD, 3 * local), ((0, PADDED - SHARD), (0, 0)))
    everywhere = jnp.broadcast_to(qkv[None], (8,) + qkv.shape)
    qkv_z = lax.all_to_all(everywhere, Z, 0, 0, tiled=True)
    blocks = four_blocks(kernel_order(own_tokens), "tp")

    starts = stream_starts(segment_ids[0])
    own_first = piece * rows
    own_start = lax.dynamic_slice_in_dim(starts, own_first, rows)
    position = own_first + jnp.arange(rows, dtype=jnp.int32) - own_start
    frequency = jnp.exp(-math.log(10000.0) * jnp.arange(HD // 2, dtype=F32) * 2.0 / HD)
    angles = frequency[:, None] * position.astype(F32)[None]
    window = 2 * BLOCK
    cosine, sine = jnp.cos(angles), jnp.sin(angles)
    key_start = (own_start - own_first + window)[None]
    gain = qk_scale[:, None]
    attn_step = kernel_order(attn_rate)[:, None]
    step_block = lax.dynamic_slice_in_dim(kernel_order(mlp_rate), tp * local, local)[:, None]

    wide = gate_up_weight.astype(BF16).reshape(SHARD, 2 * hidden)
    rest = jnp.concatenate(out_rows + [wide, down_weight.T.astype(BF16)], axis=1)
    rest_y = in_order(spot, 3, four_blocks(rest, "y"), (0, 1, 2, 3))

    (qkv_z,) = after([qkv_z], rest_y, cosine, sine, key_start, gain, attn_step, step_block, *blocks)
    qkv_near = four_blocks(qkv_z, "y")
    ahead, behind = shift(rest_y, Z, 8, 1), shift(rest_y, Z, 8, -1)
    (qkv_stack,) = after([jnp.stack(qkv_near)], ahead, behind)
    qkv_far = swap_core(qkv_stack)
    query, own, features, size = project(spot, blocks, qkv_near, qkv_far, gain, cosine, sine)
    before = lax.ppermute(own[:, rows - window :], ("zl", "co"), [(i, i + 1) for i in range(3)])
    attended = attention(key_start, query, before, own)
    everyone = four_blocks(attended, "tp")
    near = ring_z(rest_y, ahead, behind, {1: (qkv_far,), 2: (before,), 3: (everyone[1], everyone[3])})
    far = [swap_core(block) for block in near]
    parts, mixed = layer(
        spot, everyone, features, size, attn_step, up_scale[None], gate_scale[None], near, far
    )
    landed = lax.all_to_all(parts, "tp", 0, 0, tiled=True).astype(F32)
    mlp_block = landed[0] + landed[1] + landed[2] + landed[3]

    kept = mixed - step_block * mixed
    moved = step_block * mlp_block
    sums = jnp.stack(
        [
            jnp.sum(mlp_block * mlp_block, axis=0),
            jnp.sum(kept * kept, axis=0),
            jnp.sum(kept * moved, axis=0),
            jnp.sum(moved * moved, axis=0),
        ]
    )
    sums = sum(four_blocks(sums, "tp"))
    pull = lax.rsqrt(sums[0] + EPS)
    length = jnp.maximum(sums[1] + 2.0 * pull * sums[2] + pull * pull * sums[3], 0.0)
    final = math.sqrt(D) * lax.rsqrt(length + EPS)
    result = ((kept + pull[None] * moved) * final[None]).astype(BF16)
    return outer_order(result).T[None]


def solution(mesh):
    fine = Mesh(mesh.devices.reshape(4, 4, 4, 2, 2), ("zh", "y", "tp", "zl", "co"))
    rep, cp = ("zh", "y"), ("zl", "co")
    in_specs = (
        P(rep, cp, "tp"),
        P(rep + cp, None, "tp"),
        P("tp", rep + cp),
        P(rep + cp, None, "tp"),
        P("tp", rep + cp),
        P("tp"),
        P(),
        P(),
        P("tp"),
        P("tp"),
        P(rep, None),
    )
    return jax.shard_map(
        body, mesh=fine, in_specs=in_specs, out_specs=P(rep, cp, "tp"), check_vma=False
    )
```

```python
import functools
import math

import jax
import jax.numpy as jnp
from jax import lax
from jax.experimental import pallas as pl
from jax.experimental.pallas import tpu as pltpu
from jax.sharding import Mesh, PartitionSpec as P

D = 1280
HD = 64
EPS = 1e-06
F32 = jnp.float32
BF16 = jnp.bfloat16
Z = ("zh", "zl")
BLOCK = 256
LOG2E = 1.4426950408889634


def ring(count, step):
    return [(i, (i + step) % count) for i in range(count)]


def shift(block, axis, count, step):
    return lax.ppermute(block, axis, ring(count, step))


def swap_core(block):
    return lax.ppermute(block, "co", [(0, 1), (1, 0)])


SHARD = 20
PADDED = 24
WIDE = 64 * PADDED
RING_ORDER = (0, 7, 1, 6, 2, 5, 3, 4)
SMALL = pl.BlockSpec(memory_space=pltpu.SMEM)
NEAR = pl.BlockSpec(memory_space=pltpu.VMEM)
FAR = pl.BlockSpec(memory_space=pl.ANY)


def four_blocks(block, axis):
    return [block] + [shift(block, axis, 4, 4 - away) for away in (1, 2, 3)]


def after(blocks, *earlier):
    return list(lax.optimization_barrier((tuple(blocks), earlier))[0])


def order_kernel(which, aways, place_ref, *refs):
    count = len(aways)
    blocks, whole_ref, held = refs[:count], refs[count], refs[count + 1]
    me = place_ref[which]
    for block, away in zip(blocks, aways):
        held[(me + away) % count] = block[...]
    whole_ref[...] = jnp.concatenate([held[slot] for slot in range(count)], axis=0)


def in_order(spot, which, blocks, aways):
    rows, cols = blocks[0].shape
    count = len(blocks)
    return pl.pallas_call(
        functools.partial(order_kernel, which, aways),
        out_shape=jax.ShapeDtypeStruct((count * rows, cols), BF16),
        in_specs=[SMALL] + [NEAR] * count,
        out_specs=NEAR,
        scratch_shapes=[pltpu.VMEM((count, rows, cols), BF16)],
        cost_estimate=pl.CostEstimate(flops=0, bytes_accessed=count * rows * cols * 4, transcendentals=0),
        name="in_order",
    )(spot, *blocks)


def ring_z(start, ahead, behind, waits):
    blocks = [start]
    for step in range(1, 4):
        ahead, behind = after([ahead, behind], *waits.get(step, ()))
        blocks += [ahead, behind]
        ahead = shift(ahead, Z, 8, 1)
        if step < 3:
            behind = shift(behind, Z, 8, -1)
    return blocks + [ahead]


def chunk_squares(read, count, width):
    def step(index, total):
        wide = read(index).astype(F32)
        return total + jnp.sum((wide * wide).reshape(-1, 8, width), axis=0)

    return jnp.sum(lax.fori_loop(0, count, step, jnp.zeros((8, width), F32)), axis=0, keepdims=True)


def attend(head, heads, part, start_ref, q_ref, window, o_ref, cols):
    key_row = lax.broadcasted_iota(jnp.int32, (BLOCK, BLOCK), 0)
    query_col = lax.broadcasted_iota(jnp.int32, (BLOCK, BLOCK), 1)
    span = pl.ds(pl.multiple_of(head * HD, HD), HD)
    own = slice(part * BLOCK, (part + 1) * BLOCK)
    query = q_ref[span, own]
    start = start_ref[:, own]
    scores = []
    for step in range(3):
        base = (part + step) * BLOCK
        score = lax.dot_general(
            window(head, part + step), query, (((0,), (0,)), ((), ())), preferred_element_type=F32
        )
        allowed = key_row >= start - base
        if step == 2:
            allowed = allowed & (key_row <= query_col)
        scores.append(jnp.where(allowed, score, -1e30))
    top = jnp.maximum(jnp.maximum(scores[0], scores[1]), scores[2])
    top = jnp.max(top, axis=0, keepdims=True)
    total = jnp.zeros((1, BLOCK), F32)
    mixed = jnp.zeros((HD, BLOCK), F32)
    for step in range(3):
        weight = jnp.exp2((scores[step] - top) * (math.sqrt(HD) * LOG2E))
        total = total + jnp.sum(weight, axis=0, keepdims=True)
        mixed = mixed + jnp.dot(
            window(heads + head, part + step), weight.astype(BF16), preferred_element_type=F32
        )
    o_ref[span, cols] = (mixed / total).astype(BF16)


def window_of(own_ref, before_ref):
    def window(row, block):
        span = pl.ds(pl.multiple_of(row * HD, HD), HD)
        ref, block = (before_ref, block) if block < 2 else (own_ref, block - 2)
        return ref[span, block * BLOCK : (block + 1) * BLOCK]

    return window


def recent_kernel(start_ref, q_ref, own_ref, o_ref):
    heads = q_ref.shape[0] // HD

    def one_head(head, carry):
        attend(head, heads, 2, start_ref, q_ref, window_of(own_ref, None), o_ref, slice(0, BLOCK))
        return carry

    lax.fori_loop(0, heads, one_head, 0)


def attention_kernel(start_ref, q_ref, before_ref, own_ref, recent_ref, o_ref):
    heads = q_ref.shape[0] // HD
    o_ref[:, 2 * BLOCK :] = recent_ref[...]

    def one_head(head, carry):
        for part in range(2):
            cols = slice(part * BLOCK, (part + 1) * BLOCK)
            attend(head, heads, part, start_ref, q_ref, window_of(own_ref, before_ref), o_ref, cols)
        return carry

    lax.fori_loop(0, heads, one_head, 0)


def attention_recent(start, query, own):
    return pl.pallas_call(
        recent_kernel,
        out_shape=jax.ShapeDtypeStruct((query.shape[0], BLOCK), BF16),
        in_specs=[NEAR] * 3,
        out_specs=NEAR,
        cost_estimate=pl.CostEstimate(flops=260_000_000, bytes_accessed=2_000_000, transcendentals=1_000_000),
        name="attention_recent",
    )(start, query, own)


def attention(start, query, before, own, recent):
    return pl.pallas_call(
        attention_kernel,
        out_shape=jax.ShapeDtypeStruct(query.shape, BF16),
        in_specs=[NEAR] * 5,
        out_specs=NEAR,
        cost_estimate=pl.CostEstimate(flops=520_000_000, bytes_accessed=4_000_000, transcendentals=2_000_000),
        name="attention",
    )(start, query, before, own, recent)


def stream_starts(segment):
    order = jnp.arange(segment.shape[0], dtype=jnp.int32)
    earlier = jnp.concatenate([segment[:1], segment[:-1]])
    return lax.cummax(jnp.where(segment != earlier, order, jnp.zeros_like(order)))


def project_kernel(place_ref, *refs):
    x_refs, near_refs, far_refs, gain_ref, cos_ref, sin_ref = refs[:4], refs[4:8], refs[8], *refs[9:12]
    query_ref, own_ref, features_ref, size_ref, held, weight, result, sems = refs[12:]
    tp, core, spot_y = place_ref[0], place_ref[1], place_ref[3]
    local, rows = query_ref.shape
    copies = []
    for away, ref in enumerate(near_refs):
        y = (spot_y + away) % 4
        copies.append(pltpu.make_async_copy(ref, weight.at[:, core, y], sems.at[away]))
        copies.append(pltpu.make_async_copy(far_refs.at[away], weight.at[:, 1 - core, y], sems.at[4 + away]))
    for copy in copies:
        copy.start()
    held[...] = jnp.zeros_like(held)
    for away, ref in enumerate(x_refs):
        block = (tp + away) % 4
        features_ref[pl.ds(pl.multiple_of(block * local, local), local), :] = ref[...]
        for shard in range(16):
            held[block, shard, :SHARD] = ref[shard * SHARD : (shard + 1) * SHARD]
    size = lax.rsqrt(
        chunk_squares(lambda i: features_ref[pl.ds(pl.multiple_of(i * 128, 128), 128), :], D // 128, rows) + EPS
    )
    size_ref[...] = size
    for copy in copies:
        copy.wait()
    for kind in range(3):
        part = weight[..., kind * local : (kind + 1) * local].reshape(WIDE, local)
        turned = jnp.transpose(part)
        wide = turned.astype(F32)
        length = lax.rsqrt(jnp.sum(wide * wide, axis=1, keepdims=True) + EPS)
        raw = jnp.dot(turned, held[...].reshape(WIDE, rows), preferred_element_type=F32)
        result[kind * local : (kind + 1) * local] = raw * length * size
    half = HD // 2
    cosine, sine = cos_ref[...], sin_ref[...]

    def one_head(index, carry):
        span = pl.ds(pl.multiple_of(index * HD, HD), HD)
        gain = gain_ref[span, :]
        for kind, target in ((0, query_ref), (1, own_ref)):
            part = result[pl.ds(pl.multiple_of(kind * local + index * HD, HD), HD), :]
            length = lax.rsqrt(jnp.sum(part * part, axis=0, keepdims=True) + EPS)
            part = (gain * (part * length)).astype(BF16).astype(F32)
            first, second = part[:half], part[half:]
            both = [first * cosine - second * sine, first * sine + second * cosine]
            target[span, :] = jnp.concatenate(both, axis=0).astype(BF16)
        spot = pl.ds(pl.multiple_of(local + index * HD, HD), HD)
        own_ref[spot, :] = result[pl.ds(pl.multiple_of(2 * local + index * HD, HD), HD), :].astype(BF16)
        return carry

    lax.fori_loop(0, local // HD, one_head, 0)


def project(spot, blocks, near, far, gain, cosine, sine):
    local, rows = blocks[0].shape
    return pl.pallas_call(
        project_kernel,
        out_shape=[
            jax.ShapeDtypeStruct((local, rows), BF16),
            jax.ShapeDtypeStruct((2 * local, rows), BF16),
            jax.ShapeDtypeStruct((D, rows), BF16),
            jax.ShapeDtypeStruct((1, rows), F32),
        ],
        in_specs=[SMALL] + [NEAR] * 4 + [FAR] * 5 + [NEAR] * 3,
        out_specs=[NEAR] * 4,
        scratch_shapes=[
            pltpu.VMEM((4, 16, PADDED, rows), BF16),
            pltpu.VMEM((8, 2, 4, PADDED, 3 * local), BF16),
            pltpu.VMEM((3 * local, rows), F32),
            pltpu.SemaphoreType.DMA((8,)),
        ],
        compiler_params=pltpu.CompilerParams(vmem_limit_bytes=40 * 2**20),
        cost_estimate=pl.CostEstimate(flops=1_900_000_000, bytes_accessed=12_000_000, transcendentals=0),
        name="project",
    )(spot, *blocks, *near, far, gain, cosine, sine)


def layer_kernel(place_ref, *refs):
    a_refs, features_ref, size_ref, attn_ref, up_ref, gate_ref = refs[:4], *refs[4:9]
    near_refs, far_refs = refs[9:17], refs[17:25]
    part_ref, mixed_ref, attended, state, turned, inner, weight, sems = refs[25:]
    tp, core, ring = place_ref[0], place_ref[1], place_ref[2]
    local, rows = a_refs[0].shape
    hidden = up_ref.shape[1]
    bounds = (0, D, D + 2 * hidden, D + 3 * hidden)
    copies = []
    for kind in range(3):
        cols = slice(bounds[kind], bounds[kind + 1])
        for side, blocks in ((core, near_refs), (1 - core, far_refs)):
            for away, block in zip(RING_ORDER, blocks):
                target = weight.at[(ring + away) % 8, side, :, cols]
                copies.append(pltpu.make_async_copy(block.at[:, cols], target, sems.at[len(copies)]))
                copies[-1].start()
    for away, ref in enumerate(a_refs):
        attended[away * local : (away + 1) * local] = ref[...]
    for copy in copies[:16]:
        copy.wait()

    def group(index, cols):
        return weight[pl.ds(2 * index, 2), :, :, cols].reshape(local, -1)

    def eighth(index):
        return weight[index, :, :, :D].reshape(D // 8, D)

    out_length = lax.rsqrt(chunk_squares(eighth, 8, D) + EPS)

    def project_out(index, total):
        left = (group(index, slice(0, D)).astype(F32) * out_length).astype(BF16)
        block = jnp.dot(left, attended[...], preferred_element_type=F32)
        state[pl.ds(pl.multiple_of(index * local, local), local), :] = block
        return total + jnp.sum((block * block).reshape(-1, 8, rows), axis=0)

    zero = jnp.zeros((8, rows), F32)
    total = jnp.sum(lax.fori_loop(0, 4, project_out, zero), axis=0, keepdims=True)
    pull = lax.rsqrt(total + EPS)
    size = size_ref[...]

    def mix(index, total):
        span = pl.ds(pl.multiple_of(index * 128, 128), 128)
        before = features_ref[span, :].astype(F32) * size
        mixed = before + attn_ref[span, :] * (state[span, :] * pull - before)
        state[span, :] = mixed
        return total + jnp.sum((mixed * mixed).reshape(-1, 8, rows), axis=0)

    total = jnp.sum(lax.fori_loop(0, D // 128, mix, zero), axis=0, keepdims=True)
    scale = lax.rsqrt(total + EPS)

    def turn(index, carry):
        span = pl.ds(pl.multiple_of(index * 128, 128), 128)
        mixed = state[span, :] * scale
        state[span, :] = mixed
        turned[:, span] = jnp.transpose(mixed).astype(BF16)
        return carry

    lax.fori_loop(0, D // 128, turn, 0)
    mixed_ref[...] = state[pl.ds(pl.multiple_of(tp * local, local), local), :]
    for copy in copies[16:]:
        copy.wait()

    def columns(start, index):
        cols = pl.ds(pl.multiple_of(start + index * BLOCK, BLOCK), BLOCK)
        return weight[..., cols].reshape(D, BLOCK)

    def length(part):
        wide = part.astype(F32)
        return lax.rsqrt(jnp.sum(wide * wide, axis=0, keepdims=True) + EPS)

    def expand(index, carry):
        cols = pl.ds(pl.multiple_of(index * BLOCK, BLOCK), BLOCK)
        up_part, gate_part = columns(D, index), columns(D + hidden, index)
        up = jnp.dot(turned[...], up_part, preferred_element_type=F32)
        gate = jnp.dot(turned[...], gate_part, preferred_element_type=F32)
        up = up * (up_ref[:, cols] * length(up_part) * length(columns(D + 2 * hidden, index)))
        gate = gate * (gate_ref[:, cols] * length(gate_part) * math.sqrt(D))
        inner[:, cols] = (up * (gate / (1.0 + jnp.exp(-gate)))).astype(BF16)
        return carry

    lax.fori_loop(0, hidden // BLOCK, expand, 0)

    def contract(index, carry):
        block = lax.dot_general(
            group(index, slice(D + 2 * hidden, D + 3 * hidden)),
            inner[...],
            (((1,), (1,)), ((), ())),
            preferred_element_type=F32,
        )
        part_ref[index] = block.astype(BF16)
        return carry

    lax.fori_loop(0, 4, contract, 0)


def layer(spot, attended, features, size, attn_step, up_scale, gate_scale, near, far):
    local, rows = attended[0].shape
    hidden = up_scale.shape[1]
    return pl.pallas_call(
        layer_kernel,
        out_shape=[
            jax.ShapeDtypeStruct((4, local, rows), BF16),
            jax.ShapeDtypeStruct((local, rows), F32),
        ],
        in_specs=[SMALL] + [NEAR] * 9 + [FAR] * 16,
        out_specs=[NEAR] * 2,
        scratch_shapes=[
            pltpu.VMEM((D, rows), BF16),
            pltpu.VMEM((D, rows), F32),
            pltpu.VMEM((rows, D), BF16),
            pltpu.VMEM((rows, hidden), BF16),
            pltpu.VMEM((8, 2, 80, D + 3 * hidden), BF16),
            pltpu.SemaphoreType.DMA((48,)),
        ],
        compiler_params=pltpu.CompilerParams(vmem_limit_bytes=56 * 2**20),
        cost_estimate=pl.CostEstimate(flops=10_000_000_000, bytes_accessed=20_000_000, transcendentals=1_000_000),
        name="layer",
    )(spot, *attended, features, size, attn_step, up_scale, gate_scale, *near, *far)


def kernel_order(array):
    shape = array.shape
    parts = array.reshape((shape[0] // 320, 4, 2, 2, SHARD) + shape[1:])
    return jnp.moveaxis(parts, 1, 3).reshape(shape)


def outer_order(array):
    shape = array.shape
    parts = array.reshape((shape[0] // 320, 2, 2, 4, SHARD) + shape[1:])
    return jnp.moveaxis(parts, 3, 1).reshape(shape)


def body(
    tokens,
    qkv_weight,
    out_weight,
    gate_up_weight,
    down_weight,
    qk_scale,
    attn_rate,
    mlp_rate,
    up_scale,
    gate_scale,
    segment_ids,
):
    rows = tokens.shape[1]
    local = tokens.shape[2]
    hidden = gate_up_weight.shape[2]
    tp = lax.axis_index("tp")
    core = lax.axis_index("co")
    spot_y = lax.axis_index("y")
    piece = lax.axis_index("zl") * 2 + core
    spot_z = lax.axis_index("zh") * 2 + lax.axis_index("zl")
    spot = jnp.stack([tp, core, spot_z, spot_y]).astype(jnp.int32)

    out_rows = four_blocks(out_weight.T.astype(BF16), "tp")
    blocks = four_blocks(kernel_order(tokens[0].T), "tp")

    starts = stream_starts(segment_ids[0])
    own_first = piece * rows
    own_start = lax.dynamic_slice_in_dim(starts, own_first, rows)
    position = own_first + jnp.arange(rows, dtype=jnp.int32) - own_start
    frequency = jnp.exp(-math.log(10000.0) * jnp.arange(HD // 2, dtype=F32) * 2.0 / HD)
    angles = frequency[:, None] * position.astype(F32)[None]
    window = 2 * BLOCK
    cosine, sine = jnp.cos(angles), jnp.sin(angles)
    key_start = (own_start - own_first + window)[None]
    gain = qk_scale[:, None]
    attn_step = kernel_order(attn_rate)[:, None]
    step_block = lax.dynamic_slice_in_dim(kernel_order(mlp_rate), tp * local, local)[:, None]

    wide = gate_up_weight.astype(BF16).reshape(SHARD, 2 * hidden)
    rest = jnp.concatenate(out_rows + [wide, down_weight.T.astype(BF16)], axis=1)
    (shard,) = after([qkv_weight.astype(BF16)], rest)
    qkv = jnp.pad(shard.reshape(SHARD, 3 * local), ((0, PADDED - SHARD), (0, 0)))
    everywhere = jnp.broadcast_to(qkv[None], (8,) + qkv.shape)
    qkv_z = lax.all_to_all(everywhere, Z, 0, 0, tiled=True)
    rest_y = in_order(spot, 3, four_blocks(rest, "y"), (0, 1, 2, 3))

    (qkv_z,) = after([qkv_z], rest_y, cosine, sine, key_start, gain, attn_step, step_block, *blocks)
    qkv_near = four_blocks(qkv_z, "y")
    ahead, behind = shift(rest_y, Z, 8, 1), shift(rest_y, Z, 8, -1)
    (qkv_stack,) = after([jnp.stack(qkv_near)], ahead, behind)
    qkv_far = swap_core(qkv_stack)
    query, own, features, size = project(spot, blocks, qkv_near, qkv_far, gain, cosine, sine)
    before = lax.ppermute(own[:, rows - window :], ("zl", "co"), [(i, i + 1) for i in range(3)])
    recent = attention_recent(key_start, query, own)
    (before,) = after([before], recent)
    attended = attention(key_start, query, before, own, recent)
    everyone = four_blocks(attended, "tp")
    near = ring_z(rest_y, ahead, behind, {2: (before, recent), 3: (everyone[1], everyone[3])})
    far = [swap_core(block) for block in near]
    parts, mixed = layer(
        spot, everyone, features, size, attn_step, up_scale[None], gate_scale[None], near, far
    )
    landed = lax.all_to_all(parts, "tp", 0, 0, tiled=True).astype(F32)
    mlp_block = landed[0] + landed[1] + landed[2] + landed[3]

    kept = mixed - step_block * mixed
    moved = step_block * mlp_block
    sums = jnp.stack(
        [
            jnp.sum(mlp_block * mlp_block, axis=0),
            jnp.sum(kept * kept, axis=0),
            jnp.sum(kept * moved, axis=0),
            jnp.sum(moved * moved, axis=0),
        ]
    )
    sums = sum(four_blocks(sums, "tp"))
    pull = lax.rsqrt(sums[0] + EPS)
    length = jnp.maximum(sums[1] + 2.0 * pull * sums[2] + pull * pull * sums[3], 0.0)
    final = math.sqrt(D) * lax.rsqrt(length + EPS)
    result = ((kept + pull[None] * moved) * final[None]).astype(BF16)
    return outer_order(result).T[None]


def solution(mesh):
    fine = Mesh(mesh.devices.reshape(4, 4, 4, 2, 2), ("zh", "y", "tp", "zl", "co"))
    rep, cp = ("zh", "y"), ("zl", "co")
    in_specs = (
        P(rep, cp, "tp"),
        P(rep + cp, None, "tp"),
        P("tp", rep + cp),
        P(rep + cp, None, "tp"),
        P("tp", rep + cp),
        P("tp"),
        P(),
        P(),
        P("tp"),
        P("tp"),
        P(rep, None),
    )
    return jax.shard_map(
        body, mesh=fine, in_specs=in_specs, out_specs=P(rep, cp, "tp"), check_vma=False
    )
```

```python
import functools
import math

import jax
import jax.numpy as jnp
from jax import lax
from jax.experimental import pallas as pl
from jax.experimental.pallas import tpu as pltpu
from jax.sharding import Mesh, PartitionSpec as P

D = 1280
HD = 64
EPS = 1e-06
F32 = jnp.float32
BF16 = jnp.bfloat16
Z = ("zh", "zl")
BLOCK = 256
LOG2E = 1.4426950408889634


def ring(count, step):
    return [(i, (i + step) % count) for i in range(count)]


def shift(block, axis, count, step):
    return lax.ppermute(block, axis, ring(count, step))


def swap_core(block):
    return lax.ppermute(block, "co", [(0, 1), (1, 0)])


SHARD = 20
PADDED = 24
WIDE = 64 * PADDED
RING_ORDER = (0, 7, 1, 6, 2, 5, 3, 4)
SMALL = pl.BlockSpec(memory_space=pltpu.SMEM)
NEAR = pl.BlockSpec(memory_space=pltpu.VMEM)
FAR = pl.BlockSpec(memory_space=pl.ANY)


def four_blocks(block, axis):
    return [block] + [shift(block, axis, 4, 4 - away) for away in (1, 2, 3)]


def after(blocks, *earlier):
    return list(lax.optimization_barrier((tuple(blocks), earlier))[0])


def order_kernel(which, aways, place_ref, *refs):
    count = len(aways)
    blocks, whole_ref, held = refs[:count], refs[count], refs[count + 1]
    me = place_ref[which]
    for block, away in zip(blocks, aways):
        held[(me + away) % count] = block[...]
    whole_ref[...] = jnp.concatenate([held[slot] for slot in range(count)], axis=0)


def in_order(spot, which, blocks, aways):
    rows, cols = blocks[0].shape
    count = len(blocks)
    return pl.pallas_call(
        functools.partial(order_kernel, which, aways),
        out_shape=jax.ShapeDtypeStruct((count * rows, cols), BF16),
        in_specs=[SMALL] + [NEAR] * count,
        out_specs=NEAR,
        scratch_shapes=[pltpu.VMEM((count, rows, cols), BF16)],
        cost_estimate=pl.CostEstimate(flops=0, bytes_accessed=count * rows * cols * 4, transcendentals=0),
        name="in_order",
    )(spot, *blocks)


def ring_z(start, ahead, behind, waits):
    blocks = [start]
    for step in range(1, 4):
        ahead, behind = after([ahead, behind], *waits.get(step, ()))
        blocks += [ahead, behind]
        ahead = shift(ahead, Z, 8, 1)
        if step < 3:
            behind = shift(behind, Z, 8, -1)
    return blocks + [ahead]


def chunk_squares(read, count, width):
    def step(index, total):
        wide = read(index).astype(F32)
        return total + jnp.sum((wide * wide).reshape(-1, 8, width), axis=0)

    return jnp.sum(lax.fori_loop(0, count, step, jnp.zeros((8, width), F32)), axis=0, keepdims=True)


def attend(head, heads, part, start_ref, q_ref, window, o_ref, cols):
    key_row = lax.broadcasted_iota(jnp.int32, (BLOCK, BLOCK), 0)
    query_col = lax.broadcasted_iota(jnp.int32, (BLOCK, BLOCK), 1)
    span = pl.ds(pl.multiple_of(head * HD, HD), HD)
    own = slice(part * BLOCK, (part + 1) * BLOCK)
    query = q_ref[span, own]
    start = start_ref[:, own]
    scores = []
    for step in range(3):
        base = (part + step) * BLOCK
        score = lax.dot_general(
            window(head, part + step), query, (((0,), (0,)), ((), ())), preferred_element_type=F32
        )
        allowed = key_row >= start - base
        if step == 2:
            allowed = allowed & (key_row <= query_col)
        scores.append(jnp.where(allowed, score, -1e30))
    top = jnp.maximum(jnp.maximum(scores[0], scores[1]), scores[2])
    top = jnp.max(top, axis=0, keepdims=True)
    total = jnp.zeros((1, BLOCK), F32)
    mixed = jnp.zeros((HD, BLOCK), F32)
    for step in range(3):
        weight = jnp.exp2((scores[step] - top) * (math.sqrt(HD) * LOG2E))
        total = total + jnp.sum(weight, axis=0, keepdims=True)
        mixed = mixed + jnp.dot(
            window(heads + head, part + step), weight.astype(BF16), preferred_element_type=F32
        )
    o_ref[span, cols] = (mixed / total).astype(BF16)


def window_of(own_ref, before_ref):
    def window(row, block):
        span = pl.ds(pl.multiple_of(row * HD, HD), HD)
        ref, block = (before_ref, block) if block < 2 else (own_ref, block - 2)
        return ref[span, block * BLOCK : (block + 1) * BLOCK]

    return window


def recent_kernel(start_ref, q_ref, own_ref, o_ref):
    heads = q_ref.shape[0] // HD

    def one_head(head, carry):
        attend(head, heads, 2, start_ref, q_ref, window_of(own_ref, None), o_ref, slice(0, BLOCK))
        return carry

    lax.fori_loop(0, heads, one_head, 0)


def attention_kernel(start_ref, q_ref, before_ref, own_ref, recent_ref, o_ref):
    heads = q_ref.shape[0] // HD
    o_ref[:, 2 * BLOCK :] = recent_ref[...]

    def one_head(head, carry):
        for part in range(2):
            cols = slice(part * BLOCK, (part + 1) * BLOCK)
            attend(head, heads, part, start_ref, q_ref, window_of(own_ref, before_ref), o_ref, cols)
        return carry

    lax.fori_loop(0, heads, one_head, 0)


def attention_recent(start, query, own):
    return pl.pallas_call(
        recent_kernel,
        out_shape=jax.ShapeDtypeStruct((query.shape[0], BLOCK), BF16),
        in_specs=[NEAR] * 3,
        out_specs=NEAR,
        cost_estimate=pl.CostEstimate(flops=260_000_000, bytes_accessed=2_000_000, transcendentals=1_000_000),
        name="attention_recent",
    )(start, query, own)


def attention(start, query, before, own, recent):
    return pl.pallas_call(
        attention_kernel,
        out_shape=jax.ShapeDtypeStruct(query.shape, BF16),
        in_specs=[NEAR] * 5,
        out_specs=NEAR,
        cost_estimate=pl.CostEstimate(flops=520_000_000, bytes_accessed=4_000_000, transcendentals=2_000_000),
        name="attention",
    )(start, query, before, own, recent)


def stream_starts(segment):
    order = jnp.arange(segment.shape[0], dtype=jnp.int32)
    earlier = jnp.concatenate([segment[:1], segment[:-1]])
    return lax.cummax(jnp.where(segment != earlier, order, jnp.zeros_like(order)))


def project_kernel(place_ref, *refs):
    x_refs, near_refs, far_refs, gain_ref, cos_ref, sin_ref = refs[:4], refs[4:8], refs[8], *refs[9:12]
    query_ref, own_ref, features_ref, size_ref, held, weight, result, sems = refs[12:]
    tp, core, spot_y = place_ref[0], place_ref[1], place_ref[3]
    local, rows = query_ref.shape
    copies = []
    for away, ref in enumerate(near_refs):
        y = (spot_y + away) % 4
        copies.append(pltpu.make_async_copy(ref, weight.at[:, core, y], sems.at[away]))
        copies.append(pltpu.make_async_copy(far_refs.at[away], weight.at[:, 1 - core, y], sems.at[4 + away]))
    for copy in copies:
        copy.start()
    held[...] = jnp.zeros_like(held)
    for away, ref in enumerate(x_refs):
        block = (tp + away) % 4
        features_ref[pl.ds(pl.multiple_of(block * local, local), local), :] = ref[...]
        for shard in range(16):
            held[block, shard, :SHARD] = ref[shard * SHARD : (shard + 1) * SHARD]
    size = lax.rsqrt(
        chunk_squares(lambda i: features_ref[pl.ds(pl.multiple_of(i * 128, 128), 128), :], D // 128, rows) + EPS
    )
    size_ref[...] = size
    for copy in copies:
        copy.wait()
    for kind in range(3):
        part = weight[..., kind * local : (kind + 1) * local].reshape(WIDE, local)
        turned = jnp.transpose(part)
        wide = turned.astype(F32)
        length = lax.rsqrt(jnp.sum(wide * wide, axis=1, keepdims=True) + EPS)
        raw = jnp.dot(turned, held[...].reshape(WIDE, rows), preferred_element_type=F32)
        result[kind * local : (kind + 1) * local] = raw * length * size
    half = HD // 2
    cosine, sine = cos_ref[...], sin_ref[...]

    def one_head(index, carry):
        span = pl.ds(pl.multiple_of(index * HD, HD), HD)
        gain = gain_ref[span, :]
        for kind, target in ((0, query_ref), (1, own_ref)):
            part = result[pl.ds(pl.multiple_of(kind * local + index * HD, HD), HD), :]
            length = lax.rsqrt(jnp.sum(part * part, axis=0, keepdims=True) + EPS)
            part = (gain * (part * length)).astype(BF16).astype(F32)
            first, second = part[:half], part[half:]
            both = [first * cosine - second * sine, first * sine + second * cosine]
            target[span, :] = jnp.concatenate(both, axis=0).astype(BF16)
        spot = pl.ds(pl.multiple_of(local + index * HD, HD), HD)
        own_ref[spot, :] = result[pl.ds(pl.multiple_of(2 * local + index * HD, HD), HD), :].astype(BF16)
        return carry

    lax.fori_loop(0, local // HD, one_head, 0)


def project(spot, blocks, near, far, gain, cosine, sine):
    local, rows = blocks[0].shape
    return pl.pallas_call(
        project_kernel,
        out_shape=[
            jax.ShapeDtypeStruct((local, rows), BF16),
            jax.ShapeDtypeStruct((2 * local, rows), BF16),
            jax.ShapeDtypeStruct((D, rows), BF16),
            jax.ShapeDtypeStruct((1, rows), F32),
        ],
        in_specs=[SMALL] + [NEAR] * 4 + [FAR] * 5 + [NEAR] * 3,
        out_specs=[NEAR] * 4,
        scratch_shapes=[
            pltpu.VMEM((4, 16, PADDED, rows), BF16),
            pltpu.VMEM((8, 2, 4, PADDED, 3 * local), BF16),
            pltpu.VMEM((3 * local, rows), F32),
            pltpu.SemaphoreType.DMA((8,)),
        ],
        compiler_params=pltpu.CompilerParams(vmem_limit_bytes=40 * 2**20),
        cost_estimate=pl.CostEstimate(flops=1_900_000_000, bytes_accessed=12_000_000, transcendentals=0),
        name="project",
    )(spot, *blocks, *near, far, gain, cosine, sine)


def layer_kernel(place_ref, *refs):
    a_refs, features_ref, size_ref, attn_ref, up_ref, gate_ref = refs[:4], *refs[4:9]
    near_refs, far_refs = refs[9:17], refs[17:25]
    part_ref, mixed_ref, attended, state, turned, inner, weight, sems = refs[25:]
    tp, core, ring = place_ref[0], place_ref[1], place_ref[2]
    local, rows = a_refs[0].shape
    hidden = up_ref.shape[1]
    bounds = (0, D, D + 2 * hidden, D + 3 * hidden)
    copies = []
    for kind in range(3):
        cols = slice(bounds[kind], bounds[kind + 1])
        for side, blocks in ((core, near_refs), (1 - core, far_refs)):
            for away, block in zip(RING_ORDER, blocks):
                target = weight.at[(ring + away) % 8, side, :, cols]
                copies.append(pltpu.make_async_copy(block.at[:, cols], target, sems.at[len(copies)]))
                copies[-1].start()
    for away, ref in enumerate(a_refs):
        attended[away * local : (away + 1) * local] = ref[...]
    for copy in copies[:16]:
        copy.wait()

    def group(index, cols):
        return weight[pl.ds(2 * index, 2), :, :, cols].reshape(local, -1)

    def eighth(index):
        return weight[index, :, :, :D].reshape(D // 8, D)

    out_length = lax.rsqrt(chunk_squares(eighth, 8, D) + EPS)

    def project_out(index, total):
        left = (group(index, slice(0, D)).astype(F32) * out_length).astype(BF16)
        block = jnp.dot(left, attended[...], preferred_element_type=F32)
        state[pl.ds(pl.multiple_of(index * local, local), local), :] = block
        return total + jnp.sum((block * block).reshape(-1, 8, rows), axis=0)

    zero = jnp.zeros((8, rows), F32)
    total = jnp.sum(lax.fori_loop(0, 4, project_out, zero), axis=0, keepdims=True)
    pull = lax.rsqrt(total + EPS)
    size = size_ref[...]

    def mix(index, total):
        span = pl.ds(pl.multiple_of(index * 128, 128), 128)
        before = features_ref[span, :].astype(F32) * size
        mixed = before + attn_ref[span, :] * (state[span, :] * pull - before)
        state[span, :] = mixed
        return total + jnp.sum((mixed * mixed).reshape(-1, 8, rows), axis=0)

    total = jnp.sum(lax.fori_loop(0, D // 128, mix, zero), axis=0, keepdims=True)
    scale = lax.rsqrt(total + EPS)

    def turn(index, carry):
        span = pl.ds(pl.multiple_of(index * 128, 128), 128)
        mixed = state[span, :] * scale
        state[span, :] = mixed
        turned[:, span] = jnp.transpose(mixed).astype(BF16)
        return carry

    lax.fori_loop(0, D // 128, turn, 0)
    mixed_ref[...] = state[pl.ds(pl.multiple_of(tp * local, local), local), :]
    for copy in copies[16:]:
        copy.wait()

    def columns(start, index):
        cols = pl.ds(pl.multiple_of(start + index * BLOCK, BLOCK), BLOCK)
        return weight[..., cols].reshape(D, BLOCK)

    def length(part):
        wide = part.astype(F32)
        return lax.rsqrt(jnp.sum(wide * wide, axis=0, keepdims=True) + EPS)

    def expand(index, carry):
        cols = pl.ds(pl.multiple_of(index * BLOCK, BLOCK), BLOCK)
        up_part, gate_part = columns(D, index), columns(D + hidden, index)
        up = jnp.dot(turned[...], up_part, preferred_element_type=F32)
        gate = jnp.dot(turned[...], gate_part, preferred_element_type=F32)
        up = up * (up_ref[:, cols] * length(up_part) * length(columns(D + 2 * hidden, index)))
        gate = gate * (gate_ref[:, cols] * length(gate_part) * math.sqrt(D))
        inner[:, cols] = (up * (gate / (1.0 + jnp.exp(-gate)))).astype(BF16)
        return carry

    lax.fori_loop(0, hidden // BLOCK, expand, 0)

    def contract(index, carry):
        block = lax.dot_general(
            group(index, slice(D + 2 * hidden, D + 3 * hidden)),
            inner[...],
            (((1,), (1,)), ((), ())),
            preferred_element_type=F32,
        )
        part_ref[index] = block.astype(BF16)
        return carry

    lax.fori_loop(0, 4, contract, 0)


def layer(spot, attended, features, size, attn_step, up_scale, gate_scale, near, far):
    local, rows = attended[0].shape
    hidden = up_scale.shape[1]
    return pl.pallas_call(
        layer_kernel,
        out_shape=[
            jax.ShapeDtypeStruct((4, local, rows), BF16),
            jax.ShapeDtypeStruct((local, rows), F32),
        ],
        in_specs=[SMALL] + [NEAR] * 9 + [FAR] * 16,
        out_specs=[NEAR] * 2,
        scratch_shapes=[
            pltpu.VMEM((D, rows), BF16),
            pltpu.VMEM((D, rows), F32),
            pltpu.VMEM((rows, D), BF16),
            pltpu.VMEM((rows, hidden), BF16),
            pltpu.VMEM((8, 2, 80, D + 3 * hidden), BF16),
            pltpu.SemaphoreType.DMA((48,)),
        ],
        compiler_params=pltpu.CompilerParams(vmem_limit_bytes=56 * 2**20),
        cost_estimate=pl.CostEstimate(flops=10_000_000_000, bytes_accessed=20_000_000, transcendentals=1_000_000),
        name="layer",
    )(spot, *attended, features, size, attn_step, up_scale, gate_scale, *near, *far)


def kernel_order(array):
    shape = array.shape
    parts = array.reshape((shape[0] // 320, 4, 2, 2, SHARD) + shape[1:])
    return jnp.moveaxis(parts, 1, 3).reshape(shape)


def outer_order(array):
    shape = array.shape
    parts = array.reshape((shape[0] // 320, 2, 2, 4, SHARD) + shape[1:])
    return jnp.moveaxis(parts, 3, 1).reshape(shape)


def body(
    tokens,
    qkv_weight,
    out_weight,
    gate_up_weight,
    down_weight,
    qk_scale,
    attn_rate,
    mlp_rate,
    up_scale,
    gate_scale,
    segment_ids,
):
    rows = tokens.shape[1]
    local = tokens.shape[2]
    hidden = gate_up_weight.shape[2]
    tp = lax.axis_index("tp")
    core = lax.axis_index("co")
    spot_y = lax.axis_index("y")
    piece = lax.axis_index("zl") * 2 + core
    spot_z = lax.axis_index("zh") * 2 + lax.axis_index("zl")
    spot = jnp.stack([tp, core, spot_z, spot_y]).astype(jnp.int32)

    out_rows = four_blocks(out_weight.T.astype(BF16), "tp")
    blocks = four_blocks(kernel_order(tokens[0].T), "tp")

    starts = stream_starts(segment_ids[0])
    own_first = piece * rows
    own_start = lax.dynamic_slice_in_dim(starts, own_first, rows)
    position = own_first + jnp.arange(rows, dtype=jnp.int32) - own_start
    frequency = jnp.exp(-math.log(10000.0) * jnp.arange(HD // 2, dtype=F32) * 2.0 / HD)
    angles = frequency[:, None] * position.astype(F32)[None]
    window = 2 * BLOCK
    cosine, sine = jnp.cos(angles), jnp.sin(angles)
    key_start = (own_start - own_first + window)[None]
    gain = qk_scale[:, None]
    attn_step = kernel_order(attn_rate)[:, None]
    step_block = lax.dynamic_slice_in_dim(kernel_order(mlp_rate), tp * local, local)[:, None]

    wide = gate_up_weight.astype(BF16).reshape(SHARD, 2 * hidden)
    rest = jnp.concatenate(out_rows + [wide, down_weight.T.astype(BF16)], axis=1)
    (shard,) = after([qkv_weight.astype(BF16)], rest)
    qkv = jnp.pad(shard.reshape(SHARD, 3 * local), ((0, PADDED - SHARD), (0, 0)))
    everywhere = jnp.broadcast_to(qkv[None], (8,) + qkv.shape)
    qkv_z = lax.all_to_all(everywhere, Z, 0, 0, tiled=True)
    rest_y = in_order(spot, 3, four_blocks(rest, "y"), (0, 1, 2, 3))

    (qkv_z,) = after([qkv_z], rest_y, cosine, sine, key_start, gain, attn_step, step_block, *blocks)
    qkv_near = four_blocks(qkv_z, "y")
    ahead, behind = shift(rest_y, Z, 8, 1), shift(rest_y, Z, 8, -1)
    early = [swap_core(block) for block in (rest_y, ahead, behind)]
    (qkv_stack,) = after([jnp.stack(qkv_near)], ahead, behind, early[0])
    qkv_far = swap_core(qkv_stack)
    query, own, features, size = project(spot, blocks, qkv_near, qkv_far, gain, cosine, sine)
    before = lax.ppermute(own[:, rows - window :], ("zl", "co"), [(i, i + 1) for i in range(3)])
    recent = attention_recent(key_start, query, own)
    (before,) = after([before], recent, *early)
    attended = attention(key_start, query, before, own, recent)
    everyone = four_blocks(attended, "tp")
    near = ring_z(rest_y, ahead, behind, {2: (recent,), 3: (everyone[1], everyone[3])})
    (near[7],) = after([near[7]], everyone[2])
    far = early + [swap_core(block) for block in near[3:]]
    parts, mixed = layer(
        spot, everyone, features, size, attn_step, up_scale[None], gate_scale[None], near, far
    )
    landed = lax.all_to_all(parts, "tp", 0, 0, tiled=True).astype(F32)
    mlp_block = landed[0] + landed[1] + landed[2] + landed[3]

    kept = mixed - step_block * mixed
    moved = step_block * mlp_block
    sums = jnp.stack(
        [
            jnp.sum(mlp_block * mlp_block, axis=0),
            jnp.sum(kept * kept, axis=0),
            jnp.sum(kept * moved, axis=0),
            jnp.sum(moved * moved, axis=0),
        ]
    )
    sums = sum(four_blocks(sums, "tp"))
    pull = lax.rsqrt(sums[0] + EPS)
    length = jnp.maximum(sums[1] + 2.0 * pull * sums[2] + pull * pull * sums[3], 0.0)
    final = math.sqrt(D) * lax.rsqrt(length + EPS)
    result = ((kept + pull[None] * moved) * final[None]).astype(BF16)
    return outer_order(result).T[None]


def solution(mesh):
    fine = Mesh(mesh.devices.reshape(4, 4, 4, 2, 2), ("zh", "y", "tp", "zl", "co"))
    rep, cp = ("zh", "y"), ("zl", "co")
    in_specs = (
        P(rep, cp, "tp"),
        P(rep + cp, None, "tp"),
        P("tp", rep + cp),
        P(rep + cp, None, "tp"),
        P("tp", rep + cp),
        P("tp"),
        P(),
        P(),
        P("tp"),
        P("tp"),
        P(rep, None),
    )
    return jax.shard_map(
        body, mesh=fine, in_specs=in_specs, out_specs=P(rep, cp, "tp"), check_vma=False
    )
```

```python
import functools
import math

import jax
import jax.numpy as jnp
from jax import lax
from jax.experimental import pallas as pl
from jax.experimental.pallas import tpu as pltpu
from jax.sharding import Mesh, PartitionSpec as P

D = 1280
HD = 64
EPS = 1e-06
F32 = jnp.float32
BF16 = jnp.bfloat16
Z = ("zh", "zl")
BLOCK = 256
LOG2E = 1.4426950408889634


def ring(count, step):
    return [(i, (i + step) % count) for i in range(count)]


def shift(block, axis, count, step):
    return lax.ppermute(block, axis, ring(count, step))


def swap_core(block):
    return lax.ppermute(block, "co", [(0, 1), (1, 0)])


SHARD = 20
PADDED = 24
WIDE = 64 * PADDED
RING_ORDER = (0, 7, 1, 6, 2, 5, 3, 4)
SMALL = pl.BlockSpec(memory_space=pltpu.SMEM)
NEAR = pl.BlockSpec(memory_space=pltpu.VMEM)
FAR = pl.BlockSpec(memory_space=pl.ANY)


def four_blocks(block, axis):
    return [block] + [shift(block, axis, 4, 4 - away) for away in (1, 2, 3)]


def after(blocks, *earlier):
    return list(lax.optimization_barrier((tuple(blocks), earlier))[0])


def order_kernel(which, aways, place_ref, *refs):
    count = len(aways)
    blocks, whole_ref, held = refs[:count], refs[count], refs[count + 1]
    me = place_ref[which]
    for block, away in zip(blocks, aways):
        held[(me + away) % count] = block[...]
    whole_ref[...] = jnp.concatenate([held[slot] for slot in range(count)], axis=0)


def in_order(spot, which, blocks, aways):
    rows, cols = blocks[0].shape
    count = len(blocks)
    return pl.pallas_call(
        functools.partial(order_kernel, which, aways),
        out_shape=jax.ShapeDtypeStruct((count * rows, cols), BF16),
        in_specs=[SMALL] + [NEAR] * count,
        out_specs=NEAR,
        scratch_shapes=[pltpu.VMEM((count, rows, cols), BF16)],
        cost_estimate=pl.CostEstimate(flops=0, bytes_accessed=count * rows * cols * 4, transcendentals=0),
        name="in_order",
    )(spot, *blocks)


def ring_z(start, ahead, behind, waits):
    blocks = [start]
    for step in range(1, 4):
        ahead, behind = after([ahead, behind], *waits.get(step, ()))
        blocks += [ahead, behind]
        ahead = shift(ahead, Z, 8, 1)
        if step < 3:
            behind = shift(behind, Z, 8, -1)
    return blocks + [ahead]


def chunk_squares(read, count, width):
    def step(index, total):
        wide = read(index).astype(F32)
        return total + jnp.sum((wide * wide).reshape(-1, 8, width), axis=0)

    return jnp.sum(lax.fori_loop(0, count, step, jnp.zeros((8, width), F32)), axis=0, keepdims=True)


def attend(head, heads, part, start_ref, q_ref, window, o_ref, cols):
    key_row = lax.broadcasted_iota(jnp.int32, (BLOCK, BLOCK), 0)
    query_col = lax.broadcasted_iota(jnp.int32, (BLOCK, BLOCK), 1)
    span = pl.ds(pl.multiple_of(head * HD, HD), HD)
    own = slice(part * BLOCK, (part + 1) * BLOCK)
    query = q_ref[span, own]
    start = start_ref[:, own]
    scores = []
    for step in range(3):
        base = (part + step) * BLOCK
        score = lax.dot_general(
            window(head, part + step), query, (((0,), (0,)), ((), ())), preferred_element_type=F32
        )
        allowed = key_row >= start - base
        if step == 2:
            allowed = allowed & (key_row <= query_col)
        scores.append(jnp.where(allowed, score, -1e30))
    top = jnp.maximum(jnp.maximum(scores[0], scores[1]), scores[2])
    top = jnp.max(top, axis=0, keepdims=True)
    total = jnp.zeros((1, BLOCK), F32)
    mixed = jnp.zeros((HD, BLOCK), F32)
    for step in range(3):
        weight = jnp.exp2((scores[step] - top) * (math.sqrt(HD) * LOG2E))
        total = total + jnp.sum(weight, axis=0, keepdims=True)
        mixed = mixed + jnp.dot(
            window(heads + head, part + step), weight.astype(BF16), preferred_element_type=F32
        )
    o_ref[span, cols] = (mixed / total).astype(BF16)


def window_of(own_ref, before_ref):
    def window(row, block):
        span = pl.ds(pl.multiple_of(row * HD, HD), HD)
        ref, block = (before_ref, block) if block < 2 else (own_ref, block - 2)
        return ref[span, block * BLOCK : (block + 1) * BLOCK]

    return window


def recent_kernel(start_ref, q_ref, own_ref, o_ref):
    heads = q_ref.shape[0] // HD

    def one_head(head, carry):
        attend(head, heads, 2, start_ref, q_ref, window_of(own_ref, None), o_ref, slice(0, BLOCK))
        return carry

    lax.fori_loop(0, heads, one_head, 0)


def attention_kernel(start_ref, q_ref, before_ref, own_ref, recent_ref, o_ref):
    heads = q_ref.shape[0] // HD
    o_ref[:, 2 * BLOCK :] = recent_ref[...]

    def one_head(head, carry):
        for part in range(2):
            cols = slice(part * BLOCK, (part + 1) * BLOCK)
            attend(head, heads, part, start_ref, q_ref, window_of(own_ref, before_ref), o_ref, cols)
        return carry

    lax.fori_loop(0, heads, one_head, 0)


def attention_recent(start, query, own):
    return pl.pallas_call(
        recent_kernel,
        out_shape=jax.ShapeDtypeStruct((query.shape[0], BLOCK), BF16),
        in_specs=[NEAR] * 3,
        out_specs=NEAR,
        cost_estimate=pl.CostEstimate(flops=260_000_000, bytes_accessed=2_000_000, transcendentals=1_000_000),
        name="attention_recent",
    )(start, query, own)


def attention(start, query, before, own, recent):
    return pl.pallas_call(
        attention_kernel,
        out_shape=jax.ShapeDtypeStruct(query.shape, BF16),
        in_specs=[NEAR] * 5,
        out_specs=NEAR,
        cost_estimate=pl.CostEstimate(flops=520_000_000, bytes_accessed=4_000_000, transcendentals=2_000_000),
        name="attention",
    )(start, query, before, own, recent)


def stream_starts(segment):
    order = jnp.arange(segment.shape[0], dtype=jnp.int32)
    earlier = jnp.concatenate([segment[:1], segment[:-1]])
    return lax.cummax(jnp.where(segment != earlier, order, jnp.zeros_like(order)))


def project_kernel(place_ref, *refs):
    x_refs, near_refs, far_refs, gain_ref, cos_ref, sin_ref = refs[:4], refs[4:8], refs[8], *refs[9:12]
    query_ref, own_ref, features_ref, size_ref, held, weight, result, sems = refs[12:]
    tp, core, spot_y = place_ref[0], place_ref[1], place_ref[3]
    local, rows = query_ref.shape
    copies = []
    for away, ref in enumerate(near_refs):
        y = (spot_y + away) % 4
        copies.append(pltpu.make_async_copy(ref, weight.at[:, core, y], sems.at[away]))
        copies.append(pltpu.make_async_copy(far_refs.at[away], weight.at[:, 1 - core, y], sems.at[4 + away]))
    for copy in copies:
        copy.start()
    held[...] = jnp.zeros_like(held)
    for away, ref in enumerate(x_refs):
        block = (tp + away) % 4
        features_ref[pl.ds(pl.multiple_of(block * local, local), local), :] = ref[...]
        for shard in range(16):
            held[block, shard, :SHARD] = ref[shard * SHARD : (shard + 1) * SHARD]
    size = lax.rsqrt(
        chunk_squares(lambda i: features_ref[pl.ds(pl.multiple_of(i * 128, 128), 128), :], D // 128, rows) + EPS
    )
    size_ref[...] = size
    for copy in copies:
        copy.wait()
    for kind in range(3):
        part = weight[..., kind * local : (kind + 1) * local].reshape(WIDE, local)
        turned = jnp.transpose(part)
        wide = turned.astype(F32)
        length = lax.rsqrt(jnp.sum(wide * wide, axis=1, keepdims=True) + EPS)
        raw = jnp.dot(turned, held[...].reshape(WIDE, rows), preferred_element_type=F32)
        result[kind * local : (kind + 1) * local] = raw * length * size
    half = HD // 2
    cosine, sine = cos_ref[...], sin_ref[...]

    def one_head(index, carry):
        span = pl.ds(pl.multiple_of(index * HD, HD), HD)
        gain = gain_ref[span, :]
        for kind, target in ((0, query_ref), (1, own_ref)):
            part = result[pl.ds(pl.multiple_of(kind * local + index * HD, HD), HD), :]
            length = lax.rsqrt(jnp.sum(part * part, axis=0, keepdims=True) + EPS)
            part = (gain * (part * length)).astype(BF16).astype(F32)
            first, second = part[:half], part[half:]
            both = [first * cosine - second * sine, first * sine + second * cosine]
            target[span, :] = jnp.concatenate(both, axis=0).astype(BF16)
        spot = pl.ds(pl.multiple_of(local + index * HD, HD), HD)
        own_ref[spot, :] = result[pl.ds(pl.multiple_of(2 * local + index * HD, HD), HD), :].astype(BF16)
        return carry

    lax.fori_loop(0, local // HD, one_head, 0)


def project(spot, blocks, near, far, gain, cosine, sine):
    local, rows = blocks[0].shape
    return pl.pallas_call(
        project_kernel,
        out_shape=[
            jax.ShapeDtypeStruct((local, rows), BF16),
            jax.ShapeDtypeStruct((2 * local, rows), BF16),
            jax.ShapeDtypeStruct((D, rows), BF16),
            jax.ShapeDtypeStruct((1, rows), F32),
        ],
        in_specs=[SMALL] + [NEAR] * 4 + [FAR] * 5 + [NEAR] * 3,
        out_specs=[NEAR] * 4,
        scratch_shapes=[
            pltpu.VMEM((4, 16, PADDED, rows), BF16),
            pltpu.VMEM((8, 2, 4, PADDED, 3 * local), BF16),
            pltpu.VMEM((3 * local, rows), F32),
            pltpu.SemaphoreType.DMA((8,)),
        ],
        compiler_params=pltpu.CompilerParams(vmem_limit_bytes=40 * 2**20),
        cost_estimate=pl.CostEstimate(flops=1_900_000_000, bytes_accessed=12_000_000, transcendentals=0),
        name="project",
    )(spot, *blocks, *near, far, gain, cosine, sine)


def layer_kernel(place_ref, *refs):
    a_refs, features_ref, size_ref, attn_ref, up_ref, gate_ref = refs[:4], *refs[4:9]
    near_refs, far_refs = refs[9:17], refs[17:25]
    part_ref, mixed_ref, attended, state, turned, inner, weight, sems = refs[25:]
    tp, core, ring = place_ref[0], place_ref[1], place_ref[2]
    local, rows = a_refs[0].shape
    hidden = up_ref.shape[1]
    bounds = (0, D, D + 2 * hidden, D + 3 * hidden)
    copies = []
    for kind in range(3):
        cols = slice(bounds[kind], bounds[kind + 1])
        for side, blocks in ((core, near_refs), (1 - core, far_refs)):
            for away, block in zip(RING_ORDER, blocks):
                target = weight.at[(ring + away) % 8, side, :, cols]
                copies.append(pltpu.make_async_copy(block.at[:, cols], target, sems.at[len(copies)]))
                copies[-1].start()
    for away, ref in enumerate(a_refs):
        attended[away * local : (away + 1) * local] = ref[...]
    for copy in copies[:16]:
        copy.wait()

    def group(index, cols):
        return weight[pl.ds(2 * index, 2), :, :, cols].reshape(local, -1)

    def eighth(index):
        return weight[index, :, :, :D].reshape(D // 8, D)

    out_length = lax.rsqrt(chunk_squares(eighth, 8, D) + EPS)

    def project_out(index, total):
        left = (group(index, slice(0, D)).astype(F32) * out_length).astype(BF16)
        block = jnp.dot(left, attended[...], preferred_element_type=F32)
        state[pl.ds(pl.multiple_of(index * local, local), local), :] = block
        return total + jnp.sum((block * block).reshape(-1, 8, rows), axis=0)

    zero = jnp.zeros((8, rows), F32)
    total = jnp.sum(lax.fori_loop(0, 4, project_out, zero), axis=0, keepdims=True)
    pull = lax.rsqrt(total + EPS)
    size = size_ref[...]

    def mix(index, total):
        span = pl.ds(pl.multiple_of(index * 128, 128), 128)
        before = features_ref[span, :].astype(F32) * size
        mixed = before + attn_ref[span, :] * (state[span, :] * pull - before)
        state[span, :] = mixed
        return total + jnp.sum((mixed * mixed).reshape(-1, 8, rows), axis=0)

    total = jnp.sum(lax.fori_loop(0, D // 128, mix, zero), axis=0, keepdims=True)
    scale = lax.rsqrt(total + EPS)

    def turn(index, carry):
        span = pl.ds(pl.multiple_of(index * 128, 128), 128)
        mixed = state[span, :] * scale
        state[span, :] = mixed
        turned[:, span] = jnp.transpose(mixed).astype(BF16)
        return carry

    lax.fori_loop(0, D // 128, turn, 0)
    mixed_ref[...] = state[pl.ds(pl.multiple_of(tp * local, local), local), :]
    for copy in copies[16:]:
        copy.wait()

    def columns(start, index):
        cols = pl.ds(pl.multiple_of(start + index * BLOCK, BLOCK), BLOCK)
        return weight[..., cols].reshape(D, BLOCK)

    def length(part):
        wide = part.astype(F32)
        return lax.rsqrt(jnp.sum(wide * wide, axis=0, keepdims=True) + EPS)

    def expand(index, carry):
        cols = pl.ds(pl.multiple_of(index * BLOCK, BLOCK), BLOCK)
        up_part, gate_part = columns(D, index), columns(D + hidden, index)
        up = jnp.dot(turned[...], up_part, preferred_element_type=F32)
        gate = jnp.dot(turned[...], gate_part, preferred_element_type=F32)
        up = up * (up_ref[:, cols] * length(up_part) * length(columns(D + 2 * hidden, index)))
        gate = gate * (gate_ref[:, cols] * length(gate_part) * math.sqrt(D))
        inner[:, cols] = (up * (gate / (1.0 + jnp.exp(-gate)))).astype(BF16)
        return carry

    lax.fori_loop(0, hidden // BLOCK, expand, 0)

    def contract(index, carry):
        block = lax.dot_general(
            group(index, slice(D + 2 * hidden, D + 3 * hidden)),
            inner[...],
            (((1,), (1,)), ((), ())),
            preferred_element_type=F32,
        )
        part_ref[index] = block.astype(BF16)
        return carry

    lax.fori_loop(0, 4, contract, 0)


def layer(spot, attended, features, size, attn_step, up_scale, gate_scale, near, far):
    local, rows = attended[0].shape
    hidden = up_scale.shape[1]
    return pl.pallas_call(
        layer_kernel,
        out_shape=[
            jax.ShapeDtypeStruct((4, local, rows), BF16),
            jax.ShapeDtypeStruct((local, rows), F32),
        ],
        in_specs=[SMALL] + [NEAR] * 9 + [FAR] * 16,
        out_specs=[NEAR] * 2,
        scratch_shapes=[
            pltpu.VMEM((D, rows), BF16),
            pltpu.VMEM((D, rows), F32),
            pltpu.VMEM((rows, D), BF16),
            pltpu.VMEM((rows, hidden), BF16),
            pltpu.VMEM((8, 2, 80, D + 3 * hidden), BF16),
            pltpu.SemaphoreType.DMA((48,)),
        ],
        compiler_params=pltpu.CompilerParams(vmem_limit_bytes=56 * 2**20),
        cost_estimate=pl.CostEstimate(flops=10_000_000_000, bytes_accessed=20_000_000, transcendentals=1_000_000),
        name="layer",
    )(spot, *attended, features, size, attn_step, up_scale, gate_scale, *near, *far)


def kernel_order(array):
    shape = array.shape
    parts = array.reshape((shape[0] // 320, 4, 2, 2, SHARD) + shape[1:])
    return jnp.moveaxis(parts, 1, 3).reshape(shape)


def outer_order(array):
    shape = array.shape
    parts = array.reshape((shape[0] // 320, 2, 2, 4, SHARD) + shape[1:])
    return jnp.moveaxis(parts, 3, 1).reshape(shape)


def body(
    tokens,
    qkv_weight,
    out_weight,
    gate_up_weight,
    down_weight,
    qk_scale,
    attn_rate,
    mlp_rate,
    up_scale,
    gate_scale,
    segment_ids,
):
    rows = tokens.shape[1]
    local = tokens.shape[2]
    hidden = gate_up_weight.shape[2]
    tp = lax.axis_index("tp")
    core = lax.axis_index("co")
    spot_y = lax.axis_index("y")
    piece = lax.axis_index("zl") * 2 + core
    spot_z = lax.axis_index("zh") * 2 + lax.axis_index("zl")
    spot = jnp.stack([tp, core, spot_z, spot_y]).astype(jnp.int32)

    out_rows = four_blocks(out_weight.T.astype(BF16), "tp")
    blocks = four_blocks(kernel_order(tokens[0].T), "tp")

    starts = stream_starts(segment_ids[0])
    own_first = piece * rows
    own_start = lax.dynamic_slice_in_dim(starts, own_first, rows)
    position = own_first + jnp.arange(rows, dtype=jnp.int32) - own_start
    frequency = jnp.exp(-math.log(10000.0) * jnp.arange(HD // 2, dtype=F32) * 2.0 / HD)
    angles = frequency[:, None] * position.astype(F32)[None]
    window = 2 * BLOCK
    cosine, sine = jnp.cos(angles), jnp.sin(angles)
    key_start = (own_start - own_first + window)[None]
    gain = qk_scale[:, None]
    attn_step = kernel_order(attn_rate)[:, None]
    step_block = lax.dynamic_slice_in_dim(kernel_order(mlp_rate), tp * local, local)[:, None]

    wide = gate_up_weight.astype(BF16).reshape(SHARD, 2 * hidden)
    rest = jnp.concatenate(out_rows + [wide, down_weight.T.astype(BF16)], axis=1)
    (shard,) = after([qkv_weight.astype(BF16)], rest)
    qkv = jnp.pad(shard.reshape(SHARD, 3 * local), ((0, PADDED - SHARD), (0, 0)))
    everywhere = jnp.broadcast_to(qkv[None], (8,) + qkv.shape)
    qkv_z = lax.all_to_all(everywhere, Z, 0, 0, tiled=True)
    rest_y = in_order(spot, 3, four_blocks(rest, "y"), (0, 1, 2, 3))

    (qkv_z,) = after([qkv_z], rest_y, cosine, sine, key_start, gain, attn_step, step_block, *blocks)
    qkv_near = four_blocks(qkv_z, "y")
    ahead, behind = shift(rest_y, Z, 8, 1), shift(rest_y, Z, 8, -1)
    early = [swap_core(block) for block in (rest_y, ahead, behind)]
    (qkv_stack,) = after([jnp.stack(qkv_near)], ahead, behind)
    qkv_far = swap_core(qkv_stack)
    query, own, features, size = project(spot, blocks, qkv_near, qkv_far, gain, cosine, sine)
    before = lax.ppermute(own[:, rows - window :], ("zl", "co"), [(i, i + 1) for i in range(3)])
    recent = attention_recent(key_start, query, own)
    (before,) = after([before], recent)
    attended = attention(key_start, query, before, own, recent)
    everyone = four_blocks(attended, "tp")
    near = ring_z(rest_y, ahead, behind, {2: (before, recent), 3: (everyone[1], everyone[3])})
    (near[7],) = after([near[7]], everyone[2])
    far = early + [swap_core(block) for block in near[3:]]
    parts, mixed = layer(
        spot, everyone, features, size, attn_step, up_scale[None], gate_scale[None], near, far
    )
    landed = lax.all_to_all(parts, "tp", 0, 0, tiled=True).astype(F32)
    mlp_block = landed[0] + landed[1] + landed[2] + landed[3]

    kept = mixed - step_block * mixed
    moved = step_block * mlp_block
    sums = jnp.stack(
        [
            jnp.sum(mlp_block * mlp_block, axis=0),
            jnp.sum(kept * kept, axis=0),
            jnp.sum(kept * moved, axis=0),
            jnp.sum(moved * moved, axis=0),
        ]
    )
    sums = sum(four_blocks(sums, "tp"))
    pull = lax.rsqrt(sums[0] + EPS)
    length = jnp.maximum(sums[1] + 2.0 * pull * sums[2] + pull * pull * sums[3], 0.0)
    final = math.sqrt(D) * lax.rsqrt(length + EPS)
    result = ((kept + pull[None] * moved) * final[None]).astype(BF16)
    return outer_order(result).T[None]


def solution(mesh):
    fine = Mesh(mesh.devices.reshape(4, 4, 4, 2, 2), ("zh", "y", "tp", "zl", "co"))
    rep, cp = ("zh", "y"), ("zl", "co")
    in_specs = (
        P(rep, cp, "tp"),
        P(rep + cp, None, "tp"),
        P("tp", rep + cp),
        P(rep + cp, None, "tp"),
        P("tp", rep + cp),
        P("tp"),
        P(),
        P(),
        P("tp"),
        P("tp"),
        P(rep, None),
    )
    return jax.shard_map(
        body, mesh=fine, in_specs=in_specs, out_specs=P(rep, cp, "tp"), check_vma=False
    )
```
